32 devices in a mesh: groups: 2 (over x), chan: 16 (over z, y, core).
Axes of the slice: x: 2, y: 2, z: 4, core: 2. Of those that a mesh axis runs over, the one named last changes fastest.
Arguments:
- spectra: bfloat16 [256, 8, 6144], P(('groups', 'chan')), parts along dimension 0
- bad_flag: int32 [256], P(('groups', 'chan')), parts along dimension 0, may hold values 0 or 1
- source_pick: int32 [32], P(('groups', 'chan')), parts along dimension 0, may hold values from 0 to 7
- lag_start: int32 [32], P(('groups', 'chan')), parts along dimension 0, may hold values from -1000 to -23
Outputs:
- correlations: float32 [16, 256, 1024], P(None, ('groups', 'chan')), parts along dimension 1
The draws below stay inside these ranges and needn't reach their ends.
There are 2 independent parts, one for each index of `groups`. The reference program is written for one: setup_inputs(seed, part) draws one part's arguments, and reference() takes and returns one part's arrays. A program takes and returns all parts, laid end to end along the dimension named above; each array names one. Nothing has to cross between parts.
Inputs may be any that keep to these rules, and one draw needn't show every extreme that they name: Lag windows lie within -1000 to 1000: lag_start + 1023 <= 1000.
All inputs are finite; a program needn't handle non-finite values. No bound on the sum of `bad_flag` on one device may be relied on, other than what follows from the above.
Results may differ from the reference program's by a relative error of at most 0.0027.
Values may be sent and summed in bfloat16 or wider, within the bound.
No kernel may reach another device: no remote copies, remote signals or barrier semaphores. Data moves between devices by JAX's collectives and lax.ppermute only.
A program may use at most 64 MiB of HBM per device.

```python
import math
import jax
import jax.numpy as jnp
from jax import lax

CH_DEV = 8
W = 8
SRC_DEV = 1
F = 3072
NFFT = 12000
LAGW = 1024
MAXLAG = 1000
SMOOTH = 64
CHANNELS = 128
SRC = 16


def draw_spectra(key, part):
    keys = jax.random.split(key, 5)
    shape = (CHANNELS, W, 2 * F)
    noise = jax.random.normal(keys[0], shape, jnp.float32)
    bin_scale = jnp.exp(jax.random.uniform(keys[1], (CHANNELS, W, 1, F // SMOOTH, SMOOTH), jnp.float32, -1.15, 1.15))
    envelope = jnp.exp(jax.random.uniform(keys[2], (CHANNELS, W, 1, F // SMOOTH, 1), jnp.float32, -1.2, 1.2))
    shaped = noise.reshape(CHANNELS, W, 2, F // SMOOTH, SMOOTH) * bin_scale * envelope
    ramp = 1.0 + 2.0 * jnp.arange(CHANNELS, dtype=jnp.float32) / max(CHANNELS - 1, 1)
    coupling = ramp * jax.random.uniform(keys[3], (CHANNELS,), jnp.float32, 0.8, 1.2)
    common = jax.random.normal(keys[4], (W, 2 * F), jnp.float32)
    values = shaped.reshape(shape) + 1.5 * coupling[:, None, None] * common[None]
    return values.astype(jnp.bfloat16)


def plant(entries, rng, smallest, top_value):
    shape = entries.shape
    spot = [jax.random.randint(jax.random.fold_in(rng, axis), (), 0, shape[axis]) for axis in range(len(shape))]
    entries = entries.at[tuple(spot)].set(smallest)
    longest = shape.index(max(shape))
    spot[longest] = (spot[longest] + 1) % shape[longest]
    return entries.at[tuple(spot)].set(top_value)


def setup_inputs(seed: int = 0, part: int = 0) -> dict:
    streams_of = jax.random.split(jax.random.key(seed), 5)
    part_splits = jax.random.split(jax.random.fold_in(streams_of[4], part), 5)
    return {
        "spectra": draw_spectra(jax.random.fold_in(jax.random.fold_in(streams_of[4], part), 71), part),
        "bad_flag": plant((jax.random.randint(part_splits[1], (CHANNELS,), 0, 16) < 1).astype(jnp.int32), jax.random.fold_in(part_splits[1], 1), 0, 1),
        "source_pick": plant(jax.random.randint(part_splits[2], (SRC,), 0, CH_DEV), jax.random.fold_in(part_splits[2], 1), 0, CH_DEV - 1).astype(jnp.int32),
        "lag_start": plant(jax.random.randint(part_splits[3], (SRC,), 0 - MAXLAG, MAXLAG - LAGW + 2), jax.random.fold_in(part_splits[3], 1), 0 - MAXLAG, (MAXLAG - LAGW + 2) - 1).astype(jnp.int32),
    }


def build_table():
    bin_index = jnp.arange(1, F + 1, dtype=jnp.int32)
    lag_index = jnp.arange(LAGW, dtype=jnp.int32)
    turns = jnp.mod(bin_index[:, None] * lag_index[None, :], NFFT)
    angle = 2.0 * math.pi / NFFT * turns.astype(jnp.float32)
    return jnp.concatenate([jnp.cos(angle), -jnp.sin(angle)], axis=0).astype(jnp.bfloat16)

def reference(spectra, bad_flag, source_pick, lag_start):
    channel_total = lax.optimization_barrier(jnp.sum(spectra.astype(jnp.float32), axis=0))
    cleaned = spectra.astype(jnp.float32) - channel_total / CHANNELS
    blocks = cleaned.reshape(CHANNELS, W, 2, F // SMOOTH, SMOOTH)
    block_level = lax.optimization_barrier(jnp.mean(blocks[:, :, 0] ** 2 + blocks[:, :, 1] ** 2, axis=-1))
    keep = (1 - bad_flag).astype(jnp.float32)
    block_scale = keep[:, None, None] / jnp.sqrt(block_level + 1e-06)
    whitened = (blocks * block_scale[:, :, None, :, None]).reshape(CHANNELS, W, 2 * F).astype(jnp.bfloat16)
    owner_rows = jnp.arange(SRC, dtype=jnp.int32) // SRC_DEV * CH_DEV + source_pick.astype(jnp.int32)
    picked = jnp.take(whitened, owner_rows, axis=0).astype(jnp.float32)
    bin_index = jnp.arange(1, F + 1, dtype=jnp.int32)
    turns = jnp.mod(bin_index[None, :] * lag_start[:, None].astype(jnp.int32), NFFT)
    angle = 2.0 * math.pi / NFFT * turns.astype(jnp.float32)
    cosine = jnp.cos(angle)[:, None, :]
    sine_part = jnp.sin(angle)[:, None, :]
    real_src = picked[..., :F]
    imag_src = picked[..., F:]
    shifted = jnp.concatenate([real_src * cosine + imag_src * sine_part, imag_src * cosine - real_src * sine_part], axis=-1).astype(jnp.bfloat16)
    lag_table = build_table()
    receivers = whitened.astype(jnp.float32)
    real_rec = receivers[..., :F]
    imag_rec = receivers[..., F:]
    norm_factor = 1.0 / math.sqrt(W * F)

    def one_source(source_row):
        source_row = source_row.astype(jnp.float32)
        real_s = source_row[:, :F]
        imag_s = source_row[:, F:]
        cross_re = jnp.einsum('wf,rwf->rf', real_s, real_rec) + jnp.einsum('wf,rwf->rf', imag_s, imag_rec)
        cross_im = jnp.einsum('wf,rwf->rf', real_s, imag_rec) - jnp.einsum('wf,rwf->rf', imag_s, real_rec)
        cross = (jnp.concatenate([cross_re, cross_im], axis=-1) * norm_factor).astype(jnp.bfloat16)
        return jnp.dot(cross, lag_table, preferred_element_type=jnp.float32)
    return lax.map(one_source, shifted)
```

```python
import functools
import math

import jax
import jax.numpy as jnp
import ml_dtypes
import numpy as np
from jax import lax
from jax.experimental import pallas as pl
from jax.experimental.pallas import tpu as pltpu
from jax.sharding import PartitionSpec as P

NFFT = 12000
LAGW = 1024
SMOOTH = 64
LANES = 128
SPLIT = 4
LAGS = LAGW // SPLIT
VMEM = pl.BlockSpec(memory_space=pltpu.VMEM)
SMEM = pl.BlockSpec(memory_space=pltpu.SMEM)
f32 = jnp.float32
bf16 = jnp.bfloat16


def lag_tables(bins):
    k = np.arange(1, bins + 1, dtype=np.int64)
    angle = 2.0 * np.pi / NFFT * np.mod(k[:, None] * np.arange(LAGS)[None, :], NFFT)
    both = np.stack([np.cos(angle), -np.sin(angle)]).reshape(2, bins // LANES, LANES, LAGS)
    table = both.transpose(1, 0, 2, 3).reshape(2 * bins, LAGS).astype(ml_dtypes.bfloat16)
    turn = 2.0 * np.pi / NFFT * np.mod(k[None, :] * (LAGS * np.arange(SPLIT))[:, None], NFFT)
    return table, np.stack([np.cos(turn), np.sin(turn)]).astype(np.float32)


def orders(owners):
    bits = [1 << i for i in range(owners.bit_length() - 1)]
    far = bits[:0:-1]
    other = far[:-2] + far[-2:][::-1]
    return bits[1:], far + [1], other + [1]


def masks(order):
    out = [0]
    for bit in order:
        out = out + [m ^ bit for m in out]
    return out


def swap(value, bit):
    owners = lax.axis_size("chan")
    return lax.ppermute(value, "chan", [(i, i ^ bit) for i in range(owners)])


def prepare(bins, info, spectra, own, other, first, second):
    core, pick, lag = info[0], info[1], info[2]
    half = bins // 2
    keep = (1 - info[3 + pick]).astype(f32)
    for h, dest in ((0, first), (1, second)):
        for part in range(2):
            src = pl.ds(part * bins + h * half, half)
            total = spectra[0, :, src].astype(f32)
            for r in range(1, spectra.shape[0]):
                total = total + spectra[r, :, src].astype(f32)
            cols = pl.ds(part * half, half)

            @pl.when(core == h)
            def _():
                own[:, cols] = total

            @pl.when(core != h)
            def _():
                other[:, cols] = total

            dest[:, cols] = spectra[pick, :, src]
    row = lax.broadcasted_iota(jnp.int32, (8, LANES), 0)
    high = lax.shift_right_arithmetic(lag, 5)
    low = lag - high * 32
    extra = jnp.where(
        row == 0, high.astype(f32), jnp.where(row == 1, low.astype(f32), keep)
    )
    first[:, pl.ds(bins, LANES)] = extra.astype(bf16)


def cos_sin(turns):
    whole = jnp.floor(turns * (1.0 / NFFT) + 0.5)
    rest = turns - whole * NFFT
    quarter = jnp.floor(rest * (4.0 / NFFT) + 0.5)
    phi = (rest - quarter * (NFFT / 4)) * (2.0 * math.pi / NFFT)
    sq = phi * phi
    s = phi * (1.0 + sq * (-1 / 6 + sq * (1 / 120 + sq * (-1 / 5040))))
    c = 1.0 + sq * (-0.5 + sq * (1 / 24 + sq * (-1 / 720 + sq * (1 / 40320))))
    swapped = jnp.abs(quarter) == 1.0
    cos_neg = (quarter == 1.0) | (jnp.abs(quarter) == 2.0)
    sin_neg = (quarter == -1.0) | (jnp.abs(quarter) == 2.0)
    cosine = jnp.where(swapped, s, c)
    sine = jnp.where(swapped, c, s)
    return jnp.where(cos_neg, -cosine, cosine), jnp.where(sin_neg, -sine, sine)


def correlate(
    bins, order_a, order_b, channels, info, spectra, keep, own, other, got_a, got_b, table, turn,
    out, rec, src, ang, cross,
):
    core, me = info[0], info[11]
    receivers, windows = spectra.shape[0], spectra.shape[1]
    sources = got_a.shape[0]
    half = bins // 2
    chunks = half // LANES
    norm = 1.0 / math.sqrt(windows * bins)
    rows = receivers * windows + sources * windows
    block_i = lax.broadcasted_iota(jnp.int32, (LANES, LANES), 0) // SMOOTH
    block_j = lax.broadcasted_iota(jnp.int32, (LANES, LANES), 1) // SMOOTH
    same = jnp.where(block_i == block_j, 1.0, 0.0).astype(bf16)
    masks_a, masks_b = masks(order_a), masks(order_b)
    place_b = [masks_a.index(m) for m in masks_b]
    lane = lax.broadcasted_iota(jnp.int32, (1, LANES), 1)
    inv = 1.0 / channels

    def whiten(re, im, keeps):
        count = re.shape[0]
        power = (re * re + im * im).reshape(count * windows, LANES)
        high = power.astype(bf16)
        low = (power - high.astype(f32)).astype(bf16)
        level = jnp.dot(high, same, preferred_element_type=f32) + jnp.dot(
            low, same, preferred_element_type=f32
        )
        scale = lax.rsqrt(level * (1.0 / SMOOTH) + 1e-6).reshape(count, windows, LANES) * keeps
        return (re * scale).astype(bf16).astype(f32), (im * scale).astype(bf16).astype(f32)

    tail = got_a[:, :, pl.ds(bins, LANES)].astype(f32)
    lags = tail[:, 0:1, :] * 32.0 + tail[:, 1:2, :]
    keep_src = jnp.broadcast_to(tail[:, 2:3, :], (sources, windows, LANES))

    for h, got, where in ((0, got_a, list(range(sources))), (1, got_b, place_b)):
        if h == 0:
            lag_rows, keep_rows = lags, keep_src
        else:
            lag_rows = jnp.concatenate([lags[p : p + 1] for p in where], 0)
            keep_rows = jnp.concatenate([keep_src[p : p + 1] for p in where], 0)

        def chunk(c, _):
            off = pl.multiple_of(c * LANES, LANES)
            re_at = pl.ds(off, LANES)
            im_at = pl.ds(pl.multiple_of(half + c * LANES, LANES), LANES)
            mean = []
            for at in (re_at, im_at):
                mean.append(
                    jnp.where(core == h, own[:, at], other[:, at]) * inv
                )
            x_re = spectra[:, :, pl.ds(pl.multiple_of(h * half + c * LANES, LANES), LANES)]
            x_im = spectra[:, :, pl.ds(pl.multiple_of(bins + h * half + c * LANES, LANES), LANES)]
            r_re, r_im = whiten(
                x_re.astype(f32) - mean[0][None], x_im.astype(f32) - mean[1][None], keep[...]
            )
            rec[0] = r_re
            rec[1] = r_im
            s_re, s_im = whiten(
                got[:, :, re_at].astype(f32) - mean[0][None],
                got[:, :, im_at].astype(f32) - mean[1][None],
                keep_rows,
            )
            k = (lane + (h * half + 1) + c * LANES).astype(f32)
            cosine, sine = cos_sin(lag_rows * k[None])
            src[0] = (s_re * cosine + s_im * sine).astype(bf16).astype(f32)
            src[1] = (s_im * cosine - s_re * sine).astype(bf16).astype(f32)
            a = [rec[0, :, w, :] for w in range(windows)]
            b = [rec[1, :, w, :] for w in range(windows)]
            turns = [
                (turn[0, q : q + 1, pl.ds(pl.multiple_of(h * half + c * LANES, LANES), LANES)],
                 turn[1, q : q + 1, pl.ds(pl.multiple_of(h * half + c * LANES, LANES), LANES)])
                for q in range(SPLIT)
            ]
            col = pl.multiple_of(c * 2 * LANES, LANES)
            for p in range(0, sources, 2):
                pair = []
                for i in (p, p + 1):
                    c_re = c_im = None
                    for w in range(windows):
                        g = jnp.broadcast_to(src[0, i, w : w + 1, :], (receivers, LANES))
                        e = jnp.broadcast_to(src[1, i, w : w + 1, :], (receivers, LANES))
                        t_re = g * a[w] + e * b[w]
                        t_im = g * b[w] - e * a[w]
                        c_re = t_re if c_re is None else c_re + t_re
                        c_im = t_im if c_im is None else c_im + t_im
                    pair.append((c_re * norm, c_im * norm))
                for q in range(SPLIT):
                    done = []
                    for c_re, c_im in pair:
                        if q == 0:
                            done.append((c_re, c_im))
                        else:
                            ct, st = turns[q]
                            done.append((c_re * ct - c_im * st, c_re * st + c_im * ct))
                    for part in range(2):
                        for j, i in enumerate((p, p + 1)):
                            at = q * sources * receivers + where[i] * receivers
                            cross[at : at + receivers, pl.ds(pl.multiple_of(col + part * LANES, LANES), LANES)] = done[j][part]
            return 0

        lax.fori_loop(0, chunks, chunk, 0)
        for q in range(SPLIT):
            span = sources * receivers
            part = jnp.dot(
                cross[q * span : (q + 1) * span, :].astype(bf16),
                table[h * bins : (h + 1) * bins, :],
                preferred_element_type=f32,
            )
            for p in range(sources):
                source = jnp.bitwise_xor(me, masks_a[p])
                rows_p = part[p * receivers : (p + 1) * receivers, :]
                cols = pl.ds(q * LAGS, LAGS)
                if h == 0:
                    out[source, :, cols] = rows_p
                else:
                    out[source, :, cols] = out[source, :, cols] + rows_p


def shards(spectra, bad_flag, source_pick, lag_start):
    receivers, windows, width_both = spectra.shape
    bins = width_both // 2
    owners = lax.axis_size("chan")
    half = bins // 2
    me = lax.axis_index("chan").astype(jnp.int32)
    info = jnp.concatenate(
        [jnp.stack([me & 1, source_pick[0], lag_start[0]]), bad_flag, me[None]]
    )
    keep = jnp.broadcast_to(
        (1 - bad_flag).astype(f32)[:, None, None], (receivers, windows, LANES)
    )
    own, other, first, second = pl.pallas_call(
        functools.partial(prepare, bins),
        out_shape=(
            jax.ShapeDtypeStruct((windows, bins), f32),
            jax.ShapeDtypeStruct((windows, bins), f32),
            jax.ShapeDtypeStruct((windows, bins + LANES), bf16),
            jax.ShapeDtypeStruct((windows, bins), bf16),
        ),
        in_specs=[SMEM, VMEM],
        out_specs=(VMEM,) * 4,
        compiler_params=pltpu.CompilerParams(vmem_limit_bytes=16 << 20),
        name="prepare",
    )(info, spectra)
    near, order_a, order_b = orders(owners)
    total = own + swap(other, 1)
    got_a, got_b = first[None], second[None]
    for i in range(len(order_a)):
        got_a = jnp.concatenate([got_a, swap(got_a, order_a[i])], 0)
        got_b = jnp.concatenate([got_b, swap(got_b, order_b[i])], 0)
    for bit in near:
        total = total + swap(total, bit)
    rest = swap(total, 1)
    table, turn = lag_tables(bins)
    sources = owners
    return pl.pallas_call(
        functools.partial(correlate, bins, order_a, order_b, receivers * owners),
        out_shape=jax.ShapeDtypeStruct((sources, receivers, LAGW), f32),
        in_specs=[SMEM] + [VMEM] * 8,
        out_specs=VMEM,
        scratch_shapes=[
            pltpu.VMEM((2, receivers, windows, LANES), f32),
            pltpu.VMEM((2, sources, windows, LANES), f32),
            pltpu.VMEM((8, LANES), f32),
            pltpu.VMEM((SPLIT * sources * receivers, bins), f32),
        ],
        compiler_params=pltpu.CompilerParams(vmem_limit_bytes=56 << 20),
        name="correlate",
    )(info, spectra, keep, total, rest, got_a, got_b, jnp.asarray(table), jnp.asarray(turn))


def solution(mesh):
    in_specs = (
        P(("groups", "chan"), None, None),
        P(("groups", "chan")),
        P(("groups", "chan")),
        P(("groups", "chan")),
    )
    out_specs = P(None, ("groups", "chan"), None)
    return jax.shard_map(shards, mesh=mesh, in_specs=in_specs, out_specs=out_specs, check_vma=False)
```

```python
import functools
import math

import jax
import jax.numpy as jnp
import ml_dtypes
import numpy as np
from jax import lax
from jax.experimental import pallas as pl
from jax.experimental.pallas import tpu as pltpu
from jax.sharding import PartitionSpec as P

NFFT = 12000
LAGW = 1024
SMOOTH = 64
LANES = 128
SPLIT = 4
LAGS = LAGW // SPLIT
VMEM = pl.BlockSpec(memory_space=pltpu.VMEM)
SMEM = pl.BlockSpec(memory_space=pltpu.SMEM)
f32 = jnp.float32
bf16 = jnp.bfloat16


def lag_tables(bins):
    k = np.arange(1, bins + 1, dtype=np.int64)
    angle = 2.0 * np.pi / NFFT * np.mod(k[:, None] * np.arange(LAGS)[None, :], NFFT)
    both = np.stack([np.cos(angle), -np.sin(angle)]).reshape(2, bins // LANES, LANES, LAGS)
    table = both.transpose(1, 0, 2, 3).reshape(2 * bins, LAGS).astype(ml_dtypes.bfloat16)
    turn = 2.0 * np.pi / NFFT * np.mod(k[None, :] * (LAGS * np.arange(SPLIT))[:, None], NFFT)
    return table, np.stack([np.cos(turn), np.sin(turn)]).astype(np.float32)


def orders(owners):
    bits = [1 << i for i in range(owners.bit_length() - 1)]
    far = bits[:0:-1]
    other = far[:-2] + far[-2:][::-1]
    return bits[1:], (far + [1], other + [1])


def masks(order):
    out = [0]
    for bit in order:
        out = out + [m ^ bit for m in out]
    return out


def swap(value, bit):
    owners = lax.axis_size("chan")
    return lax.ppermute(value, "chan", [(i, i ^ bit) for i in range(owners)])


def prepare(bins, source_pick, lag_start, bad_flag, spectra, *outs):
    core = lax.axis_index("chan") & 1
    pick, lag = source_pick[0], lag_start[0]
    half = bins // 2
    keep = (1 - bad_flag[pick]).astype(f32)
    row = lax.broadcasted_iota(jnp.int32, (spectra.shape[1], LANES), 0)
    high = lax.shift_right_arithmetic(lag, 5)
    low = lag - high * 32
    extra = jnp.where(row == 0, high.astype(f32), jnp.where(row == 1, low.astype(f32), keep))
    for h in range(2):
        own, other, rows = outs[3 * h : 3 * h + 3]
        for part in range(2):
            src = pl.ds(part * bins + h * half, half)
            total = spectra[0, :, src].astype(f32)
            for r in range(1, spectra.shape[0]):
                total = total + spectra[r, :, src].astype(f32)

            @pl.when(core == part)
            def _():
                own[...] = total

            @pl.when(core != part)
            def _():
                other[...] = total

            rows[0, :, pl.ds(part * half, half)] = spectra[pick, :, src]
        rows[0, :, pl.ds(bins, LANES)] = extra.astype(bf16)


def cos_sin(turns):
    whole = jnp.floor(turns * (1.0 / NFFT) + 0.5)
    rest = turns - whole * NFFT
    quarter = jnp.floor(rest * (4.0 / NFFT) + 0.5)
    phi = (rest - quarter * (NFFT / 4)) * (2.0 * math.pi / NFFT)
    sq = phi * phi
    s = phi * (1.0 + sq * (-1 / 6 + sq * (1 / 120 + sq * (-1 / 5040))))
    c = 1.0 + sq * (-0.5 + sq * (1 / 24 + sq * (-1 / 720 + sq * (1 / 40320))))
    swapped = jnp.abs(quarter) == 1.0
    cos_neg = (quarter == 1.0) | (jnp.abs(quarter) == 2.0)
    sin_neg = (quarter == -1.0) | (jnp.abs(quarter) == 2.0)
    cosine = jnp.where(swapped, s, c)
    sine = jnp.where(swapped, c, s)
    return jnp.where(cos_neg, -cosine, cosine), jnp.where(sin_neg, -sine, sine)


def correlate(h, bins, order_a, order, channels, bad_flag, spectra, own, other, got, table, turn, *rest):
    if h == 0:
        out, rec, src, ang, cross = rest
        before = None
    else:
        before, out, rec, src, ang, cross = rest
    me = lax.axis_index("chan").astype(jnp.int32)
    core = me & 1
    receivers, windows = spectra.shape[0], spectra.shape[1]
    sources = got.shape[0]
    half = bins // 2
    chunks = half // LANES
    span = sources * receivers
    norm = 1.0 / math.sqrt(windows * bins)
    block_i = lax.broadcasted_iota(jnp.int32, (LANES, LANES), 0) // SMOOTH
    block_j = lax.broadcasted_iota(jnp.int32, (LANES, LANES), 1) // SMOOTH
    same = jnp.where(block_i == block_j, 1.0, 0.0).astype(bf16)
    lane = lax.broadcasted_iota(jnp.int32, (1, LANES), 1)
    inv = 1.0 / channels
    places, seen = masks(order_a), masks(order)
    held = [seen.index(m) for m in places]
    keep = [(1 - bad_flag[r]).astype(f32) for r in range(receivers)]
    tail = got[:, :, pl.ds(bins, LANES)].astype(f32)
    lags = tail[:, 0, :] * 32.0 + tail[:, 1, :]

    def scales(power):
        count = power.shape[0]
        power = power.reshape(count * windows, LANES)
        high = power.astype(bf16)
        low = (power - high.astype(f32)).astype(bf16)
        level = jnp.dot(high, same, preferred_element_type=f32) + jnp.dot(
            low, same, preferred_element_type=f32
        )
        return lax.rsqrt(level * (1.0 / SMOOTH) + 1e-6).reshape(count, windows, LANES)

    def chunk(c, _):
        re_at = pl.ds(pl.multiple_of(c * LANES, LANES), LANES)
        im_at = pl.ds(pl.multiple_of(half + c * LANES, LANES), LANES)
        bin_at = pl.ds(pl.multiple_of(h * half + c * LANES, LANES), LANES)
        imag_at = pl.ds(pl.multiple_of(bins + h * half + c * LANES, LANES), LANES)
        m_own, m_other = own[:, re_at] * inv, other[:, re_at] * inv
        m_re = jnp.where(core == 0, m_own, m_other)
        m_im = jnp.where(core == 0, m_other, m_own)
        x_re = spectra[:, :, bin_at].astype(f32) - m_re[None]
        x_im = spectra[:, :, imag_at].astype(f32) - m_im[None]
        scale = scales(x_re * x_re + x_im * x_im)
        for r in range(receivers):
            factor = scale[r] * keep[r]
            rec[0, r] = (x_re[r] * factor).astype(bf16).astype(f32)
            rec[1, r] = (x_im[r] * factor).astype(bf16).astype(f32)
        k = (lane + (h * half + 1) + c * LANES).astype(f32)
        ang[0], ang[1] = cos_sin(lags * k)
        g_re = got[:, :, re_at].astype(f32) - m_re[None]
        g_im = got[:, :, im_at].astype(f32) - m_im[None]
        scale = scales(g_re * g_re + g_im * g_im)
        for i in range(sources):
            factor = scale[i] * jnp.broadcast_to(tail[i, 2:3, :], (windows, LANES))
            w_re = (g_re[i] * factor).astype(bf16).astype(f32)
            w_im = (g_im[i] * factor).astype(bf16).astype(f32)
            cosine = jnp.broadcast_to(ang[0, i : i + 1, :], (windows, LANES))
            sine = jnp.broadcast_to(ang[1, i : i + 1, :], (windows, LANES))
            src[0, i] = (w_re * cosine + w_im * sine).astype(bf16).astype(f32)
            src[1, i] = (w_im * cosine - w_re * sine).astype(bf16).astype(f32)
        a = [rec[0, :, w, :] for w in range(windows)]
        b = [rec[1, :, w, :] for w in range(windows)]
        turns = [(turn[0, q : q + 1, bin_at], turn[1, q : q + 1, bin_at]) for q in range(SPLIT)]
        for p in range(0, sources, 2):
            pair = []
            for i in (held[p], held[p + 1]):
                c_re = c_im = None
                for w in range(windows):
                    g = jnp.broadcast_to(src[0, i, w : w + 1, :], (receivers, LANES))
                    e = jnp.broadcast_to(src[1, i, w : w + 1, :], (receivers, LANES))
                    t_re = g * a[w] + e * b[w]
                    t_im = g * b[w] - e * a[w]
                    c_re = t_re if c_re is None else c_re + t_re
                    c_im = t_im if c_im is None else c_im + t_im
                pair.append((c_re * norm, c_im * norm))
            p_re = jnp.concatenate([pair[0][0], pair[1][0]], 0)
            p_im = jnp.concatenate([pair[0][1], pair[1][1]], 0)
            for q in range(SPLIT):
                ct, st = turns[q]
                done = (p_re, p_im) if q == 0 else (p_re * ct - p_im * st, p_re * st + p_im * ct)
                at = q * span + p * receivers
                for part in range(2):
                    cols = pl.ds(pl.multiple_of((2 * c + part) * LANES, LANES), LANES)
                    cross[at : at + 2 * receivers, cols] = done[part].astype(bf16)
        return 0

    lax.fori_loop(0, chunks, chunk, 0)
    product = jnp.dot(cross[...], table[...], preferred_element_type=f32)
    if h == 0:
        out[...] = product
        return
    product = product + before[...]
    for p in range(sources):
        source = jnp.bitwise_xor(me, places[p])
        for q in range(SPLIT):
            at = q * span + p * receivers
            out[source, :, q * LAGS : (q + 1) * LAGS] = product[at : at + receivers, :]


def shards(spectra, bad_flag, source_pick, lag_start):
    receivers, windows, width_both = spectra.shape
    bins = width_both // 2
    owners = lax.axis_size("chan")
    half = bins // 2
    flat = jax.ShapeDtypeStruct((windows, half), f32)
    rows = jax.ShapeDtypeStruct((1, windows, bins + LANES), bf16)
    ready = pl.pallas_call(
        functools.partial(prepare, bins),
        out_shape=(flat, flat, rows) * 2,
        in_specs=[SMEM, SMEM, SMEM, VMEM],
        out_specs=(VMEM,) * 6,
        compiler_params=pltpu.CompilerParams(vmem_limit_bytes=16 << 20),
        name="prepare",
    )(source_pick, lag_start, bad_flag, spectra)
    near, order = orders(owners)
    table, turn = lag_tables(bins)
    whole = SPLIT * owners * receivers
    result = ()
    for h in range(2):
        own, other, got = ready[3 * h : 3 * h + 3]
        total = own + swap(other, 1)
        for bit in near:
            total = total + swap(total, bit)
        rest = swap(total, 1)
        for bit in order[h]:
            got = jnp.concatenate([got, swap(got, bit)], 0)
        shape = (whole, LAGS) if h == 0 else (owners, receivers, LAGW)
        result = (pl.pallas_call(
            functools.partial(correlate, h, bins, order[0], order[h], receivers * owners),
            out_shape=jax.ShapeDtypeStruct(shape, f32),
            in_specs=[SMEM] + [VMEM] * (6 + h),
            out_specs=VMEM,
            scratch_shapes=[
                pltpu.VMEM((2, receivers, windows, LANES), f32),
                pltpu.VMEM((2, owners, windows, LANES), f32),
                pltpu.VMEM((2, owners, LANES), f32),
                pltpu.VMEM((whole, bins), bf16),
            ],
            compiler_params=pltpu.CompilerParams(vmem_limit_bytes=30 << 20),
            cost_estimate=pl.CostEstimate(flops=6 * 10**9, bytes_accessed=6 << 20, transcendentals=0),
            name="correlate",
        )(bad_flag, spectra, total, rest, got, jnp.asarray(table[h * bins : (h + 1) * bins]), jnp.asarray(turn), *result),)
    return result[0]


def solution(mesh):
    in_specs = (
        P(("groups", "chan"), None, None),
        P(("groups", "chan")),
        P(("groups", "chan")),
        P(("groups", "chan")),
    )
    out_specs = P(None, ("groups", "chan"), None)
    return jax.shard_map(shards, mesh=mesh, in_specs=in_specs, out_specs=out_specs, check_vma=False)
```

```python
import functools
import math

import jax
import jax.numpy as jnp
import ml_dtypes
import numpy as np
from jax import lax
from jax.experimental import pallas as pl
from jax.experimental.pallas import tpu as pltpu
from jax.sharding import PartitionSpec as P

NFFT = 12000
LAGW = 1024
SMOOTH = 64
LANES = 128
UNROLL = 3
VMEM = pl.BlockSpec(memory_space=pltpu.VMEM)
SMEM = pl.BlockSpec(memory_space=pltpu.SMEM)
HBM = pl.BlockSpec(memory_space=pltpu.HBM)
f32 = jnp.float32
bf16 = jnp.bfloat16


def lag_table(bins):
    k = np.arange(1, bins + 1, dtype=np.int64)
    angle = 2.0 * np.pi / NFFT * np.mod(k[:, None] * np.arange(LAGW)[None, :], NFFT)
    both = np.stack([np.cos(angle), -np.sin(angle)]).reshape(2, bins // LANES, LANES, LAGW)
    return both.transpose(1, 0, 2, 3).reshape(2 * bins, LAGW).astype(ml_dtypes.bfloat16)


def orders(owners):
    bits = [1 << i for i in range(owners.bit_length() - 1)]
    far = bits[:0:-1]
    other = far[-1:] + far[:-1]
    return (bits[1:], bits[1:]), (far + [1], other + [1])


def masks(order):
    out = [0]
    for bit in order:
        out = out + [m ^ bit for m in out]
    return out


def swap(value, bit):
    owners = lax.axis_size("chan")
    return lax.ppermute(value, "chan", [(i, i ^ bit) for i in range(owners)])


def prepare(bins, source_pick, lag_start, bad_flag, spectra, *rest):
    outs, (held, flags, sems, flag_sem) = rest[:6], rest[6:]
    core = lax.axis_index("chan") & 1
    pick, lag = source_pick[0], lag_start[0]
    half = bins // 2
    copies = []
    for h in range(2):
        for part in range(2):
            src = pl.ds(part * bins + h * half, half)
            slot = 2 * h + part
            copies.append(pltpu.make_async_copy(spectra.at[:, :, src], held.at[slot], sems.at[slot]))
    flag_copy = pltpu.make_async_copy(bad_flag, flags, flag_sem)
    flag_copy.start()
    for copy in copies:
        copy.start()
    row = lax.broadcasted_iota(jnp.int32, (spectra.shape[1], LANES), 0)
    high = lax.shift_right_arithmetic(lag, 5)
    low = lag - high * 32
    flag_copy.wait()
    keep = (1 - flags[pick]).astype(f32)
    extra = jnp.where(row == 0, high.astype(f32), jnp.where(row == 1, low.astype(f32), keep))
    for h in range(2):
        own, other, rows = outs[3 * h : 3 * h + 3]
        rows[0, :, pl.ds(bins, LANES)] = extra.astype(bf16)
        for part in range(2):
            slot = 2 * h + part
            copies[slot].wait()
            total = held[slot, 0].astype(f32)
            for r in range(1, held.shape[1]):
                total = total + held[slot, r].astype(f32)

            @pl.when(core == part)
            def _():
                own[...] = total

            @pl.when(core != part)
            def _():
                other[...] = total

            rows[0, :, pl.ds(part * half, half)] = held[slot, pick]


def cos_sin(turns):
    whole = jnp.floor(turns * (1.0 / NFFT) + 0.5)
    rest = turns - whole * NFFT
    quarter = jnp.floor(rest * (4.0 / NFFT) + 0.5)
    phi = (rest - quarter * (NFFT / 4)) * (2.0 * math.pi / NFFT)
    sq = phi * phi
    s = phi * (1.0 + sq * (-1 / 6 + sq * (1 / 120 + sq * (-1 / 5040))))
    c = 1.0 + sq * (-0.5 + sq * (1 / 24 + sq * (-1 / 720 + sq * (1 / 40320))))
    swapped = jnp.abs(quarter) == 1.0
    cos_neg = (quarter == 1.0) | (jnp.abs(quarter) == 2.0)
    sin_neg = (quarter == -1.0) | (jnp.abs(quarter) == 2.0)
    cosine = jnp.where(swapped, s, c)
    sine = jnp.where(swapped, c, s)
    return jnp.where(cos_neg, -cosine, cosine), jnp.where(sin_neg, -sine, sine)


def correlate(h, bins, order, first_order, channels, bad_flag, spectra, own, other, got, table, *rest):
    before, (out, rec, src, ang, cross) = rest[:h], rest[h:]
    me = lax.axis_index("chan").astype(jnp.int32)
    core = me & 1
    receivers, windows = spectra.shape[0], spectra.shape[1]
    sources = got.shape[0]
    half = bins // 2
    chunks = half // LANES
    norm = 1.0 / math.sqrt(windows * bins)
    block_i = lax.broadcasted_iota(jnp.int32, (LANES, LANES), 0) // SMOOTH
    block_j = lax.broadcasted_iota(jnp.int32, (LANES, LANES), 1) // SMOOTH
    same = jnp.where(block_i == block_j, 1.0 / SMOOTH, 0.0).astype(bf16)
    lane = lax.broadcasted_iota(jnp.int32, (1, LANES), 1)
    inv = 1.0 / channels
    places, seen = masks(first_order), masks(order)
    held = [seen.index(m) for m in places]
    keep = [(1 - bad_flag[r]).astype(f32) for r in range(receivers)]
    tail = got[:, :, pl.ds(bins, LANES)].astype(f32)
    lags = tail[:, 0, :] * 32.0 + tail[:, 1, :]

    def scales(power):
        count = power.shape[0]
        power = power.reshape(count * windows, LANES)
        high = power.astype(bf16)
        low = (power - high.astype(f32)).astype(bf16)
        level = jnp.dot(high, same, preferred_element_type=f32) + jnp.dot(
            low, same, preferred_element_type=f32
        )
        return lax.rsqrt(level + 1e-6).reshape(count, windows, LANES)

    def rounded(value):
        return value.astype(bf16).astype(f32)

    def chunk(c, _):
        re_at = pl.ds(pl.multiple_of(c * LANES, LANES), LANES)
        im_at = pl.ds(pl.multiple_of(half + c * LANES, LANES), LANES)
        bin_at = pl.ds(pl.multiple_of(h * half + c * LANES, LANES), LANES)
        imag_at = pl.ds(pl.multiple_of(bins + h * half + c * LANES, LANES), LANES)
        m_own, m_other = own[:, re_at] * inv, other[:, re_at] * inv
        m_re = jnp.where(core == 0, m_own, m_other)
        m_im = jnp.where(core == 0, m_other, m_own)
        x_re = spectra[:, :, bin_at].astype(f32) - m_re[None]
        x_im = spectra[:, :, imag_at].astype(f32) - m_im[None]
        scale = scales(x_re * x_re + x_im * x_im)
        for r in range(receivers):
            factor = scale[r] * keep[r]
            rec[0, r] = rounded(x_re[r] * factor)
            rec[1, r] = rounded(x_im[r] * factor)
        k = (lane + (h * half + 1) + c * LANES).astype(f32)
        ang[0], ang[1] = cos_sin(lags * k)
        g_re = got[:, :, re_at].astype(f32) - m_re[None]
        g_im = got[:, :, im_at].astype(f32) - m_im[None]
        scale = scales(g_re * g_re + g_im * g_im)
        for i in range(sources):
            factor = scale[i] * jnp.broadcast_to(tail[i, 2:3, :], (windows, LANES))
            w_re = rounded(g_re[i] * factor)
            w_im = rounded(g_im[i] * factor)
            cosine = ang[0, pl.ds(i, windows, stride=0), :]
            sine = ang[1, pl.ds(i, windows, stride=0), :]
            src[0, i] = rounded(w_re * cosine + w_im * sine)
            src[1, i] = rounded(w_im * cosine - w_re * sine)
        a = [rec[0, :, w, :] for w in range(windows)]
        b = [rec[1, :, w, :] for w in range(windows)]
        for p in range(0, sources, 2):
            pair = []
            for i in (held[p], held[p + 1]):
                c_re = c_im = None
                for w in range(windows):
                    g = src[0, i, pl.ds(w, receivers, stride=0), :]
                    e = src[1, i, pl.ds(w, receivers, stride=0), :]
                    t_re = g * a[w] + e * b[w]
                    t_im = g * b[w] - e * a[w]
                    c_re = t_re if c_re is None else c_re + t_re
                    c_im = t_im if c_im is None else c_im + t_im
                pair.append((c_re * norm, c_im * norm))
            for part in range(2):
                cols = pl.ds(pl.multiple_of((2 * c + part) * LANES, LANES), LANES)
                both = jnp.concatenate([pair[0][part], pair[1][part]], 0)
                cross[p * receivers : (p + 2) * receivers, cols] = both.astype(bf16)
        return 0

    lax.fori_loop(0, chunks, chunk, 0, unroll=UNROLL)
    product = jnp.dot(cross[...], table[...], preferred_element_type=f32)
    if h == 0:
        out[...] = product
        return
    product = product + before[0][...]
    for p in range(sources):
        source = jnp.bitwise_xor(me, places[p])
        out[source] = product[p * receivers : (p + 1) * receivers, :]


def shards(spectra, bad_flag, source_pick, lag_start):
    receivers, windows, width_both = spectra.shape
    bins = width_both // 2
    owners = lax.axis_size("chan")
    half = bins // 2
    flat = jax.ShapeDtypeStruct((windows, half), f32)
    rows = jax.ShapeDtypeStruct((1, windows, bins + LANES), bf16)
    ready = pl.pallas_call(
        functools.partial(prepare, bins),
        out_shape=(flat, flat, rows) * 2,
        in_specs=[SMEM, SMEM, HBM, HBM],
        out_specs=(VMEM,) * 6,
        scratch_shapes=[
            pltpu.VMEM((4, receivers, windows, half), bf16),
            pltpu.SMEM((receivers,), jnp.int32),
            pltpu.SemaphoreType.DMA((4,)),
            pltpu.SemaphoreType.DMA(()),
        ],
        compiler_params=pltpu.CompilerParams(vmem_limit_bytes=16 << 20),
        name="prepare",
    )(source_pick, lag_start, bad_flag, spectra)
    total_order, row_order = orders(owners)
    table = lag_table(bins)
    totals, gots = [], []
    for h in range(2):
        own, other, got = ready[3 * h : 3 * h + 3]
        total = own + swap(other, 1)
        for bit in total_order[h]:
            total = total + swap(total, bit)
        totals.append((total, swap(total, 1)))
        for bit in row_order[h]:
            got = jnp.concatenate([got, swap(got, bit)], 0)
        gots.append(got)
    result = ()
    for h in range(2):
        shape = (owners * receivers, LAGW) if h == 0 else (owners, receivers, LAGW)
        result = (pl.pallas_call(
            functools.partial(correlate, h, bins, row_order[h], row_order[0], receivers * owners),
            out_shape=jax.ShapeDtypeStruct(shape, f32),
            in_specs=[SMEM] + [VMEM] * (5 + h),
            out_specs=VMEM,
            scratch_shapes=[
                pltpu.VMEM((2, receivers, windows, LANES), f32),
                pltpu.VMEM((2, owners, windows, LANES), f32),
                pltpu.VMEM((2, owners, LANES), f32),
                pltpu.VMEM((owners * receivers, bins), bf16),
            ],
            compiler_params=pltpu.CompilerParams(vmem_limit_bytes=24 << 20),
            cost_estimate=pl.CostEstimate(flops=5 * 10**9, bytes_accessed=10 << 20, transcendentals=0),
            name="correlate",
        )(bad_flag, spectra, *totals[h], gots[h], jnp.asarray(table[h * bins : (h + 1) * bins]), *result),)
    return result[0]


def solution(mesh):
    in_specs = (
        P(("groups", "chan"), None, None),
        P(("groups", "chan")),
        P(("groups", "chan")),
        P(("groups", "chan")),
    )
    out_specs = P(None, ("groups", "chan"), None)
    return jax.shard_map(shards, mesh=mesh, in_specs=in_specs, out_specs=out_specs, check_vma=False)
```

```python
import functools
import math

import jax
import jax.numpy as jnp
import ml_dtypes
import numpy as np
from jax import lax
from jax.experimental import pallas as pl
from jax.experimental.pallas import tpu as pltpu
from jax.sharding import PartitionSpec as P

NFFT = 12000
LAGW = 1024
SMOOTH = 64
LANES = 128
UNROLL = 3
VMEM = pl.BlockSpec(memory_space=pltpu.VMEM)
SMEM = pl.BlockSpec(memory_space=pltpu.SMEM)
HBM = pl.BlockSpec(memory_space=pltpu.HBM)
f32 = jnp.float32
bf16 = jnp.bfloat16


def lag_table(bins):
    k = np.arange(1, bins + 1, dtype=np.int64)
    angle = 2.0 * np.pi / NFFT * np.mod(k[:, None] * np.arange(LAGW)[None, :], NFFT)
    both = np.stack([np.cos(angle), -np.sin(angle)]).reshape(2, bins // LANES, LANES, LAGW)
    return both.transpose(1, 0, 2, 3).reshape(2 * bins, LAGW).astype(ml_dtypes.bfloat16)


def orders(owners):
    bits = [1 << i for i in range(owners.bit_length() - 1)]
    near, far = bits[1:], bits[:0:-1]
    totals = near[1::-1] + near[2:], near[-1:] + near[:-1]
    return totals, (far + [1], far[-1:] + far[:-1] + [1])


def masks(order):
    out = [0]
    for bit in order:
        out = out + [m ^ bit for m in out]
    return out


def swap(value, bit):
    owners = lax.axis_size("chan")
    return lax.ppermute(value, "chan", [(i, i ^ bit) for i in range(owners)])


def pick_rows(bins, source_pick, lag_start, bad_flag, spectra, first, second, flags, sems):
    half = bins // 2
    pick, lag = source_pick[0], lag_start[0]
    copies = [pltpu.make_async_copy(bad_flag, flags, sems.at[4])]
    for h, rows in enumerate((first, second)):
        for part in range(2):
            copies.append(
                pltpu.make_async_copy(
                    spectra.at[pick, :, pl.ds(part * bins + h * half, half)],
                    rows.at[0, :, pl.ds(part * half, half)],
                    sems.at[2 * h + part],
                )
            )
    for copy in copies:
        copy.start()
    row = lax.broadcasted_iota(jnp.int32, (spectra.shape[1], LANES), 0)
    high = lax.shift_right_arithmetic(lag, 5)
    low = lag - high * 32
    copies[0].wait()
    keep = (1 - flags[pick]).astype(f32)
    extra = jnp.where(row == 0, high.astype(f32), jnp.where(row == 1, low.astype(f32), keep))
    for rows in (first, second):
        rows[0, :, pl.ds(bins, LANES)] = extra.astype(bf16)
    for copy in copies[1:]:
        copy.wait()


def add_channels(bins, spectra, *outs):
    core = lax.axis_index("chan") & 1
    half = bins // 2
    for h in range(2):
        own, other = outs[2 * h : 2 * h + 2]
        for part in range(2):
            src = pl.ds(part * bins + h * half, half)
            total = spectra[0, :, src].astype(f32)
            for r in range(1, spectra.shape[0]):
                total = total + spectra[r, :, src].astype(f32)

            @pl.when(core == part)
            def _():
                own[...] = total

            @pl.when(core != part)
            def _():
                other[...] = total


def cos_sin(turns):
    whole = jnp.floor(turns * (1.0 / NFFT) + 0.5)
    rest = turns - whole * NFFT
    quarter = jnp.floor(rest * (4.0 / NFFT) + 0.5)
    phi = (rest - quarter * (NFFT / 4)) * (2.0 * math.pi / NFFT)
    sq = phi * phi
    s = phi * (1.0 + sq * (-1 / 6 + sq * (1 / 120 + sq * (-1 / 5040))))
    c = 1.0 + sq * (-0.5 + sq * (1 / 24 + sq * (-1 / 720 + sq * (1 / 40320))))
    swapped = jnp.abs(quarter) == 1.0
    cos_neg = (quarter == 1.0) | (jnp.abs(quarter) == 2.0)
    sin_neg = (quarter == -1.0) | (jnp.abs(quarter) == 2.0)
    cosine = jnp.where(swapped, s, c)
    sine = jnp.where(swapped, c, s)
    return jnp.where(cos_neg, -cosine, cosine), jnp.where(sin_neg, -sine, sine)


def correlate(h, bins, order, first_order, channels, bad_flag, spectra, own, other, got, table, *rest):
    before, (out, rec, src, ang, cross) = rest[:h], rest[h:]
    me = lax.axis_index("chan").astype(jnp.int32)
    core = me & 1
    receivers, windows = spectra.shape[0], spectra.shape[1]
    sources = got.shape[0]
    half = bins // 2
    chunks = half // LANES
    norm = 1.0 / math.sqrt(windows * bins)
    block_i = lax.broadcasted_iota(jnp.int32, (LANES, LANES), 0) // SMOOTH
    block_j = lax.broadcasted_iota(jnp.int32, (LANES, LANES), 1) // SMOOTH
    same = jnp.where(block_i == block_j, 1.0 / SMOOTH, 0.0).astype(bf16)
    lane = lax.broadcasted_iota(jnp.int32, (1, LANES), 1)
    inv = 1.0 / channels
    places, seen = masks(first_order), masks(order)
    held = [seen.index(m) for m in places]
    keep = [(1 - bad_flag[r]).astype(f32) for r in range(receivers)]
    tail = got[:, :, pl.ds(bins, LANES)].astype(f32)
    lags = tail[:, 0, :] * 32.0 + tail[:, 1, :]
    kept = tail[:, 2, :]

    def scales(power):
        count = power.shape[0]
        power = power.reshape(count * windows, LANES)
        high = power.astype(bf16)
        low = (power - high.astype(f32)).astype(bf16)
        level = jnp.dot(high, same, preferred_element_type=f32) + jnp.dot(
            low, same, preferred_element_type=f32
        )
        return lax.rsqrt(level + 1e-6).reshape(count, windows, LANES)

    def rounded(value):
        return value.astype(bf16).astype(f32)

    def chunk(c, _):
        re_at = pl.ds(pl.multiple_of(c * LANES, LANES), LANES)
        im_at = pl.ds(pl.multiple_of(half + c * LANES, LANES), LANES)
        bin_at = pl.ds(pl.multiple_of(h * half + c * LANES, LANES), LANES)
        imag_at = pl.ds(pl.multiple_of(bins + h * half + c * LANES, LANES), LANES)
        m_own, m_other = own[:, re_at] * inv, other[:, re_at] * inv
        m_re = jnp.where(core == 0, m_own, m_other)
        m_im = jnp.where(core == 0, m_other, m_own)
        x_re = spectra[:, :, bin_at].astype(f32) - m_re[None]
        x_im = spectra[:, :, imag_at].astype(f32) - m_im[None]
        scale = scales(x_re * x_re + x_im * x_im)
        for r in range(receivers):
            factor = scale[r] * keep[r]
            rec[0, r] = rounded(x_re[r] * factor)
            rec[1, r] = rounded(x_im[r] * factor)
        k = (lane + (h * half + 1) + c * LANES).astype(f32)
        cosine, sine = cos_sin(lags * k)
        ang[0], ang[1] = cosine * kept, sine * kept
        g_re = got[:, :, re_at].astype(f32) - m_re[None]
        g_im = got[:, :, im_at].astype(f32) - m_im[None]
        scale = scales(g_re * g_re + g_im * g_im)
        for i in range(sources):
            w_re = rounded(g_re[i] * scale[i])
            w_im = rounded(g_im[i] * scale[i])
            cosine = ang[0, pl.ds(i, windows, stride=0), :]
            sine = ang[1, pl.ds(i, windows, stride=0), :]
            src[0, i] = rounded(w_re * cosine + w_im * sine)
            src[1, i] = rounded(w_im * cosine - w_re * sine)
        a = [rec[0, :, w, :] for w in range(windows)]
        b = [rec[1, :, w, :] for w in range(windows)]
        for p in range(0, sources, 2):
            pair = []
            for i in (held[p], held[p + 1]):
                c_re = c_im = None
                for w in range(windows):
                    g = src[0, i, pl.ds(w, receivers, stride=0), :]
                    e = src[1, i, pl.ds(w, receivers, stride=0), :]
                    t_re = g * a[w] + e * b[w]
                    t_im = g * b[w] - e * a[w]
                    c_re = t_re if c_re is None else c_re + t_re
                    c_im = t_im if c_im is None else c_im + t_im
                pair.append((c_re * norm, c_im * norm))
            for part in range(2):
                cols = pl.ds(pl.multiple_of((2 * c + part) * LANES, LANES), LANES)
                both = jnp.concatenate([pair[0][part], pair[1][part]], 0)
                cross[p * receivers : (p + 2) * receivers, cols] = both.astype(bf16)
        return 0

    lax.fori_loop(0, chunks, chunk, 0, unroll=UNROLL)
    product = jnp.dot(cross[...], table[...], preferred_element_type=f32)
    if h == 0:
        out[...] = product
        return
    product = product + before[0][...]
    for p in range(sources):
        source = jnp.bitwise_xor(me, places[p])
        out[source] = product[p * receivers : (p + 1) * receivers, :]


def shards(spectra, bad_flag, source_pick, lag_start):
    receivers, windows, width_both = spectra.shape
    bins = width_both // 2
    owners = lax.axis_size("chan")
    half = bins // 2
    flat = jax.ShapeDtypeStruct((windows, half), f32)
    rows = jax.ShapeDtypeStruct((1, windows, bins + LANES), bf16)
    first, second = pl.pallas_call(
        functools.partial(pick_rows, bins),
        out_shape=(rows, rows),
        in_specs=[SMEM, SMEM, HBM, HBM],
        out_specs=(VMEM, VMEM),
        scratch_shapes=[pltpu.SMEM((receivers,), jnp.int32), pltpu.SemaphoreType.DMA((5,))],
        compiler_params=pltpu.CompilerParams(vmem_limit_bytes=8 << 20),
        name="pick_rows",
    )(
        source_pick,
        lag_start,
        pltpu.with_memory_space_constraint(bad_flag, pltpu.HBM),
        pltpu.with_memory_space_constraint(spectra, pltpu.HBM),
    )
    sums = pl.pallas_call(
        functools.partial(add_channels, bins),
        out_shape=(flat,) * 4,
        in_specs=[VMEM],
        out_specs=(VMEM,) * 4,
        compiler_params=pltpu.CompilerParams(vmem_limit_bytes=8 << 20),
        name="add_channels",
    )(spectra)
    total_order, row_order = orders(owners)
    table = lag_table(bins)
    totals, gots = [], []
    for h in range(2):
        own, other = sums[2 * h : 2 * h + 2]
        got = (first, second)[h]
        total = own + swap(other, 1)
        for bit in total_order[h]:
            total = total + swap(total, bit)
        totals.append((total, swap(total, 1)))
        for bit in row_order[h]:
            got = jnp.concatenate([got, swap(got, bit)], 0)
        gots.append(got)
    result = ()
    for h in range(2):
        shape = (owners * receivers, LAGW) if h == 0 else (owners, receivers, LAGW)
        result = (pl.pallas_call(
            functools.partial(correlate, h, bins, row_order[h], row_order[0], receivers * owners),
            out_shape=jax.ShapeDtypeStruct(shape, f32),
            in_specs=[SMEM] + [VMEM] * (5 + h),
            out_specs=VMEM,
            scratch_shapes=[
                pltpu.VMEM((2, receivers, windows, LANES), f32),
                pltpu.VMEM((2, owners, windows, LANES), f32),
                pltpu.VMEM((2, owners, LANES), f32),
                pltpu.VMEM((owners * receivers, bins), bf16),
            ],
            compiler_params=pltpu.CompilerParams(vmem_limit_bytes=24 << 20),
            cost_estimate=pl.CostEstimate(flops=5 * 10**9, bytes_accessed=10 << 20, transcendentals=0),
            name="correlate",
        )(bad_flag, spectra, *totals[h], gots[h], jnp.asarray(table[h * bins : (h + 1) * bins]), *result),)
    return result[0]


def solution(mesh):
    in_specs = (
        P(("groups", "chan"), None, None),
        P(("groups", "chan")),
        P(("groups", "chan")),
        P(("groups", "chan")),
    )
    out_specs = P(None, ("groups", "chan"), None)
    return jax.shard_map(shards, mesh=mesh, in_specs=in_specs, out_specs=out_specs, check_vma=False)
```

```python
import functools
import math

import jax
import jax.numpy as jnp
import ml_dtypes
import numpy as np
from jax import lax
from jax.experimental import pallas as pl
from jax.experimental.pallas import tpu as pltpu
from jax.sharding import PartitionSpec as P

NFFT = 12000
LAGW = 1024
SMOOTH = 64
LANES = 128
UNROLL = 3
PIECES = 4
BEGIN = 3 * 10**9
VMEM = pl.BlockSpec(memory_space=pltpu.VMEM)
SMEM = pl.BlockSpec(memory_space=pltpu.SMEM)
HBM = pl.BlockSpec(memory_space=pltpu.HBM)
f32 = jnp.float32
bf16 = jnp.bfloat16


def lag_table(bins):
    k = np.arange(1, bins + 1, dtype=np.int64)
    angle = 2.0 * np.pi / NFFT * np.mod(k[:, None] * np.arange(LAGW)[None, :], NFFT)
    both = np.stack([np.cos(angle), -np.sin(angle)]).reshape(2, bins // LANES, LANES, LAGW)
    return both.transpose(1, 0, 2, 3).reshape(2 * bins, LAGW).astype(ml_dtypes.bfloat16)


def orders(owners):
    bits = [1 << i for i in range(owners.bit_length() - 1)]
    near, far = bits[1:], bits[:0:-1]
    totals = near[1::-1] + near[2:], near[-1:] + near[:-1]
    return totals, (far + [1], far[-1:] + far[:-1] + [1])


def masks(order):
    out = [0]
    for bit in order:
        out = out + [m ^ bit for m in out]
    return out


def swap(value, bit):
    owners = lax.axis_size("chan")
    return lax.ppermute(value, "chan", [(i, i ^ bit) for i in range(owners)])


def pick_rows(bins, source_pick, lag_start, bad_flag, spectra, first, second, keeps, flags, sems):
    half = bins // 2
    pick, lag = source_pick[0], lag_start[0]
    copies = [pltpu.make_async_copy(bad_flag, flags, sems.at[4])]
    for h, rows in enumerate((first, second)):
        for part in range(2):
            copies.append(
                pltpu.make_async_copy(
                    spectra.at[pick, :, pl.ds(part * bins + h * half, half)],
                    rows.at[0, :, pl.ds(part * half, half)],
                    sems.at[2 * h + part],
                )
            )
    for copy in copies:
        copy.start()
    row = lax.broadcasted_iota(jnp.int32, (spectra.shape[1], LANES), 0)
    high = lax.shift_right_arithmetic(lag, 5)
    low = lag - high * 32
    copies[0].wait()
    keep = (1 - flags[pick]).astype(f32)
    extra = jnp.where(row == 0, high.astype(f32), jnp.where(row == 1, low.astype(f32), keep))
    for rows in (first, second):
        rows[0, :, pl.ds(bins, LANES)] = extra.astype(bf16)
    for r in range(keeps.shape[0]):
        keeps[r] = jnp.full(keeps.shape[1:], (1 - flags[r]).astype(f32))
    for copy in copies[1:]:
        copy.wait()


def add_channels(bins, spectra, *outs):
    core = lax.axis_index("chan") & 1
    half = bins // 2
    outs[4][...] = spectra[...]
    for h in range(2):
        own, other = outs[2 * h : 2 * h + 2]
        for part in range(2):
            src = pl.ds(part * bins + h * half, half)
            total = spectra[0, :, src].astype(f32)
            for r in range(1, spectra.shape[0]):
                total = total + spectra[r, :, src].astype(f32)

            @pl.when(core == part)
            def _():
                own[...] = total

            @pl.when(core != part)
            def _():
                other[...] = total


def cos_sin(turns):
    whole = jnp.floor(turns * (1.0 / NFFT) + 0.5)
    rest = turns - whole * NFFT
    quarter = jnp.floor(rest * (4.0 / NFFT) + 0.5)
    phi = (rest - quarter * (NFFT / 4)) * (2.0 * math.pi / NFFT)
    sq = phi * phi
    s = phi * (1.0 + sq * (-1 / 6 + sq * (1 / 120 + sq * (-1 / 5040))))
    c = 1.0 + sq * (-0.5 + sq * (1 / 24 + sq * (-1 / 720 + sq * (1 / 40320))))
    swapped = jnp.abs(quarter) == 1.0
    cos_neg = (quarter == 1.0) | (jnp.abs(quarter) == 2.0)
    sin_neg = (quarter == -1.0) | (jnp.abs(quarter) == 2.0)
    cosine = jnp.where(swapped, s, c)
    sine = jnp.where(swapped, c, s)
    return jnp.where(cos_neg, -cosine, cosine), jnp.where(sin_neg, -sine, sine)


def rounded(value):
    return value.astype(bf16).astype(f32)


def whitening(h, bins, channels, core, own, other, windows):
    half = bins // 2
    block_i = lax.broadcasted_iota(jnp.int32, (LANES, LANES), 0) // SMOOTH
    block_j = lax.broadcasted_iota(jnp.int32, (LANES, LANES), 1) // SMOOTH
    same = jnp.where(block_i == block_j, 1.0 / SMOOTH, 0.0).astype(bf16)
    lane = lax.broadcasted_iota(jnp.int32, (1, LANES), 1)
    inv = 1.0 / channels

    def means(c):
        at = pl.ds(pl.multiple_of(c * LANES, LANES), LANES)
        m_own, m_other = own[:, at] * inv, other[:, at] * inv
        return jnp.where(core == 0, m_own, m_other), jnp.where(core == 0, m_other, m_own)

    def scales(power):
        count = power.shape[0]
        power = power.reshape(count * windows, LANES)
        high = power.astype(bf16)
        low = (power - high.astype(f32)).astype(bf16)
        level = jnp.dot(high, same, preferred_element_type=f32) + jnp.dot(
            low, same, preferred_element_type=f32
        )
        return lax.rsqrt(level + 1e-6).reshape(count, windows, LANES)

    def numbers(c):
        return (lane + (h * half + 1) + c * LANES).astype(f32)

    return means, scales, numbers


def cross_rows(c, half, mean, scales, number, got, first, lags, kept, ang, src, receivers, a, b, pairs, norm, store):
    windows = got.shape[1]
    count = got.shape[0] - first
    re_at = pl.ds(pl.multiple_of(c * LANES, LANES), LANES)
    im_at = pl.ds(pl.multiple_of(half + c * LANES, LANES), LANES)
    cosine, sine = cos_sin(lags * number)
    ang[0], ang[1] = cosine * kept, sine * kept
    g_re = got[first:, :, re_at].astype(f32) - mean[0][None]
    g_im = got[first:, :, im_at].astype(f32) - mean[1][None]
    scale = scales(g_re * g_re + g_im * g_im)
    for i in range(count):
        w_re = rounded(g_re[i] * scale[i])
        w_im = rounded(g_im[i] * scale[i])
        cosine = ang[0, pl.ds(i, windows, stride=0), :]
        sine = ang[1, pl.ds(i, windows, stride=0), :]
        src[0, i] = rounded(w_re * cosine + w_im * sine)
        src[1, i] = rounded(w_im * cosine - w_re * sine)
    for row, members in pairs:
        pair = []
        for i in members:
            c_re = c_im = None
            for w in range(windows):
                g = src[0, i - first, pl.ds(w, receivers, stride=0), :]
                e = src[1, i - first, pl.ds(w, receivers, stride=0), :]
                t_re = g * a[w] + e * b[w]
                t_im = g * b[w] - e * a[w]
                c_re = t_re if c_re is None else c_re + t_re
                c_im = t_im if c_im is None else c_im + t_im
            pair.append((c_re * norm, c_im * norm))
        for part in range(2):
            cols = pl.ds(pl.multiple_of((2 * c + part) * LANES, LANES), LANES)
            both = jnp.concatenate([pair[0][part], pair[1][part]], 0)
            store[row : row + 2 * receivers, cols] = both.astype(bf16)


def correlate(h, bins, order, first_order, channels, keep, spectra, own, other, got, table, *rest):
    before, (out, rec, src, ang, cross, *leaving) = rest[:h], rest[h:]
    me = lax.axis_index("chan").astype(jnp.int32)
    core = me & 1
    receivers, windows = spectra.shape[0], spectra.shape[1]
    sources = got.shape[0]
    half = bins // 2
    chunks = half // LANES
    norm = 1.0 / math.sqrt(windows * bins)
    block_i = lax.broadcasted_iota(jnp.int32, (LANES, LANES), 0) // SMOOTH
    block_j = lax.broadcasted_iota(jnp.int32, (LANES, LANES), 1) // SMOOTH
    same = jnp.where(block_i == block_j, 1.0 / SMOOTH, 0.0).astype(bf16)
    lane = lax.broadcasted_iota(jnp.int32, (1, LANES), 1)
    inv = 1.0 / channels
    places, seen = masks(first_order), masks(order)
    held = [seen.index(m) for m in places]
    tail = got[:, :, pl.ds(bins, LANES)].astype(f32)
    lags = tail[:, 0, :] * 32.0 + tail[:, 1, :]
    kept = tail[:, 2, :]

    def scales(power):
        count = power.shape[0]
        power = power.reshape(count * windows, LANES)
        high = power.astype(bf16)
        low = (power - high.astype(f32)).astype(bf16)
        level = jnp.dot(high, same, preferred_element_type=f32) + jnp.dot(
            low, same, preferred_element_type=f32
        )
        return lax.rsqrt(level + 1e-6).reshape(count, windows, LANES)

    def chunk(c, _):
        re_at = pl.ds(pl.multiple_of(c * LANES, LANES), LANES)
        im_at = pl.ds(pl.multiple_of(half + c * LANES, LANES), LANES)
        bin_at = pl.ds(pl.multiple_of(h * half + c * LANES, LANES), LANES)
        imag_at = pl.ds(pl.multiple_of(bins + h * half + c * LANES, LANES), LANES)
        m_own, m_other = own[:, re_at] * inv, other[:, re_at] * inv
        m_re = jnp.where(core == 0, m_own, m_other)
        m_im = jnp.where(core == 0, m_other, m_own)
        x_re = spectra[:, :, bin_at].astype(f32) - m_re[None]
        x_im = spectra[:, :, imag_at].astype(f32) - m_im[None]
        scale = scales(x_re * x_re + x_im * x_im)
        for r in range(receivers):
            factor = scale[r] * keep[r]
            rec[0, r] = rounded(x_re[r] * factor)
            rec[1, r] = rounded(x_im[r] * factor)
        k = (lane + (h * half + 1) + c * LANES).astype(f32)
        cosine, sine = cos_sin(lags * k)
        ang[0], ang[1] = cosine * kept, sine * kept
        g_re = got[:, :, re_at].astype(f32) - m_re[None]
        g_im = got[:, :, im_at].astype(f32) - m_im[None]
        scale = scales(g_re * g_re + g_im * g_im)
        for i in range(sources):
            w_re = rounded(g_re[i] * scale[i])
            w_im = rounded(g_im[i] * scale[i])
            cosine = ang[0, pl.ds(i, windows, stride=0), :]
            sine = ang[1, pl.ds(i, windows, stride=0), :]
            src[0, i] = rounded(w_re * cosine + w_im * sine)
            src[1, i] = rounded(w_im * cosine - w_re * sine)
        a = [rec[0, :, w, :] for w in range(windows)]
        b = [rec[1, :, w, :] for w in range(windows)]
        for p in range(0, sources, 2):
            pair = []
            for i in (held[p], held[p + 1]):
                c_re = c_im = None
                for w in range(windows):
                    g = src[0, i, pl.ds(w, receivers, stride=0), :]
                    e = src[1, i, pl.ds(w, receivers, stride=0), :]
                    t_re = g * a[w] + e * b[w]
                    t_im = g * b[w] - e * a[w]
                    c_re = t_re if c_re is None else c_re + t_re
                    c_im = t_im if c_im is None else c_im + t_im
                pair.append((c_re * norm, c_im * norm))
            for part in range(2):
                cols = pl.ds(pl.multiple_of((2 * c + part) * LANES, LANES), LANES)
                both = jnp.concatenate([pair[0][part], pair[1][part]], 0)
                cross[p * receivers : (p + 2) * receivers, cols] = both.astype(bf16)
        return 0

    lax.fori_loop(0, chunks, chunk, 0, unroll=UNROLL)
    if h == 0:
        out[...] = jnp.dot(cross[...], table[...], preferred_element_type=f32)
        return
    final, sems = leaving
    copies = []
    for piece in range(PIECES):
        cols = slice(piece * LAGW // PIECES, (piece + 1) * LAGW // PIECES)
        product = before[0][:, cols] + jnp.dot(
            cross[...], table[:, cols], preferred_element_type=f32
        )
        for p in range(sources):
            source = jnp.bitwise_xor(me, places[p])
            final[source, :, cols] = product[p * receivers : (p + 1) * receivers, :]
        copies.append(
            pltpu.make_async_copy(final.at[:, :, cols], out.at[:, :, cols], sems.at[piece])
        )
        copies[-1].start()
    for copy in copies:
        copy.wait()


def begin(h, bins, pairs, channels, keep, spectra, own, other, got, white, store, src, ang):
    core = lax.axis_index("chan") & 1
    receivers, windows = spectra.shape[0], spectra.shape[1]
    half = bins // 2
    norm = 1.0 / math.sqrt(windows * bins)
    means, scales, numbers = whitening(h, bins, channels, core, own, other, windows)
    tail = got[:, :, pl.ds(bins, LANES)].astype(f32)
    lags, kept = tail[:, 0, :] * 32.0 + tail[:, 1, :], tail[:, 2, :]

    def chunk(c, _):
        bin_at = pl.ds(pl.multiple_of(h * half + c * LANES, LANES), LANES)
        imag_at = pl.ds(pl.multiple_of(bins + h * half + c * LANES, LANES), LANES)
        mean = means(c)
        x_re = spectra[:, :, bin_at].astype(f32) - mean[0][None]
        x_im = spectra[:, :, imag_at].astype(f32) - mean[1][None]
        scale = scales(x_re * x_re + x_im * x_im)
        for r in range(receivers):
            factor = scale[r] * keep[r]
            white[c, 0, r] = rounded(x_re[r] * factor)
            white[c, 1, r] = rounded(x_im[r] * factor)
        a = [white[c, 0, :, w, :] for w in range(windows)]
        b = [white[c, 1, :, w, :] for w in range(windows)]
        cross_rows(
            c, half, mean, scales, numbers(c), got, 0, lags, kept, ang, src, receivers, a, b, pairs, norm, store
        )
        return 0

    lax.fori_loop(0, half // LANES, chunk, 0, unroll=UNROLL)


def finish(h, bins, first, early, pairs, places, channels, own, other, got, white, store, table, *rest):
    before, (out, src, ang, cross, *leaving) = rest[:h], rest[h:]
    me = lax.axis_index("chan").astype(jnp.int32)
    core = me & 1
    receivers, windows = white.shape[2], white.shape[3]
    half = bins // 2
    norm = 1.0 / math.sqrt(windows * bins)
    means, scales, numbers = whitening(h, bins, channels, core, own, other, windows)
    tail = got[first:, :, pl.ds(bins, LANES)].astype(f32)
    lags, kept = tail[:, 0, :] * 32.0 + tail[:, 1, :], tail[:, 2, :]
    for source, dest in early:
        cross[dest : dest + 2 * receivers, :] = store[source : source + 2 * receivers, :]

    def chunk(c, _):
        a = [white[c, 0, :, w, :] for w in range(windows)]
        b = [white[c, 1, :, w, :] for w in range(windows)]
        cross_rows(
            c, half, means(c), scales, numbers(c), got, first, lags, kept, ang, src, receivers, a, b, pairs, norm,
            cross,
        )
        return 0

    lax.fori_loop(0, half // LANES, chunk, 0, unroll=UNROLL)
    if h == 0:
        out[...] = jnp.dot(cross[...], table[...], preferred_element_type=f32)
        return
    final, sems = leaving
    copies = []
    for piece in range(PIECES):
        cols = slice(piece * LAGW // PIECES, (piece + 1) * LAGW // PIECES)
        product = before[0][:, cols] + jnp.dot(
            cross[...], table[:, cols], preferred_element_type=f32
        )
        for p, place in enumerate(places):
            source = jnp.bitwise_xor(me, place)
            final[source, :, cols] = product[p * receivers : (p + 1) * receivers, :]
        copies.append(
            pltpu.make_async_copy(final.at[:, :, cols], out.at[:, :, cols], sems.at[piece])
        )
        copies[-1].start()
    for copy in copies:
        copy.wait()


def shards(spectra, bad_flag, source_pick, lag_start):
    receivers, windows, width_both = spectra.shape
    bins = width_both // 2
    owners = lax.axis_size("chan")
    half = bins // 2
    flat = jax.ShapeDtypeStruct((windows, half), f32)
    rows = jax.ShapeDtypeStruct((1, windows, bins + LANES), bf16)
    first, second, keep = pl.pallas_call(
        functools.partial(pick_rows, bins),
        out_shape=(rows, rows, jax.ShapeDtypeStruct((receivers, windows, LANES), f32)),
        in_specs=[SMEM, SMEM, HBM, HBM],
        out_specs=(VMEM,) * 3,
        scratch_shapes=[pltpu.SMEM((receivers,), jnp.int32), pltpu.SemaphoreType.DMA((5,))],
        compiler_params=pltpu.CompilerParams(vmem_limit_bytes=8 << 20),
        name="pick_rows",
    )(
        source_pick,
        lag_start,
        pltpu.with_memory_space_constraint(bad_flag, pltpu.HBM),
        pltpu.with_memory_space_constraint(spectra, pltpu.HBM),
    )
    sums = pl.pallas_call(
        functools.partial(add_channels, bins),
        out_shape=(flat,) * 4 + (jax.ShapeDtypeStruct(spectra.shape, bf16),),
        in_specs=[VMEM],
        out_specs=(VMEM,) * 5,
        compiler_params=pltpu.CompilerParams(vmem_limit_bytes=8 << 20),
        name="add_channels",
    )(spectra)
    held_spectra = sums[4]
    total_order, row_order = orders(owners)
    table = lag_table(bins)
    channels = receivers * owners
    chunks = half // LANES
    first_count = owners // 4
    places = masks(row_order[0])
    totals, gots, begun = [], [], []
    for h in range(2):
        own, other = sums[2 * h : 2 * h + 2]
        got = (first, second)[h]
        total = own + swap(other, 1)
        for bit in total_order[h]:
            total = total + swap(total, bit)
        totals.append((total, swap(total, 1)))
        held = [masks(row_order[h]).index(m) for m in places]
        pairs = [(p * receivers, (held[p], held[p + 1])) for p in range(0, owners, 2)]
        early = [pair for pair in pairs if max(pair[1]) < first_count]
        late = [pair for pair in pairs if max(pair[1]) >= first_count]
        moved = [(2 * receivers * i, row) for i, (row, _) in enumerate(early)]
        for bit in row_order[h]:
            if h == 0 and got.shape[0] == first_count:
                begun.append(
                    (moved, late)
                    + tuple(
                        pl.pallas_call(
                            functools.partial(
                                begin, h, bins, [(2 * receivers * i, m) for i, (_, m) in enumerate(early)], channels
                            ),
                            out_shape=(
                                jax.ShapeDtypeStruct((chunks, 2, receivers, windows, LANES), f32),
                                jax.ShapeDtypeStruct((first_count * receivers, bins), bf16),
                            ),
                            in_specs=[VMEM] * 5,
                            out_specs=(VMEM, VMEM),
                            scratch_shapes=[
                                pltpu.VMEM((2, first_count, windows, LANES), f32),
                                pltpu.VMEM((2, first_count, LANES), f32),
                            ],
                            compiler_params=pltpu.CompilerParams(vmem_limit_bytes=16 << 20),
                            cost_estimate=pl.CostEstimate(flops=BEGIN, bytes_accessed=4 << 20, transcendentals=0),
                            name="begin",
                        )(keep, held_spectra, *totals[h], got)
                    )
                )
            got = jnp.concatenate([got, swap(got, bit)], 0)
        gots.append(got)
    late_count = owners - first_count
    whole = (owners * receivers, LAGW)
    moved, late, white, store = begun[0]
    part = pl.pallas_call(
        functools.partial(finish, 0, bins, first_count, moved, late, places, channels),
        out_shape=jax.ShapeDtypeStruct(whole, f32),
        in_specs=[VMEM] * 6,
        out_specs=VMEM,
        scratch_shapes=[
            pltpu.VMEM((2, late_count, windows, LANES), f32),
            pltpu.VMEM((2, late_count, LANES), f32),
            pltpu.VMEM((owners * receivers, bins), bf16),
        ],
        compiler_params=pltpu.CompilerParams(vmem_limit_bytes=16 << 20),
        cost_estimate=pl.CostEstimate(flops=4 * 10**9, bytes_accessed=10 << 20, transcendentals=0),
        name="finish",
    )(*totals[0], gots[0], white, store, jnp.asarray(table[:bins]))
    shape = (owners, receivers, LAGW)
    return pl.pallas_call(
        functools.partial(correlate, 1, bins, row_order[1], row_order[0], channels),
        out_shape=jax.ShapeDtypeStruct(shape, f32),
        in_specs=[VMEM] * 7,
        out_specs=HBM,
        scratch_shapes=[
            pltpu.VMEM((2, receivers, windows, LANES), f32),
            pltpu.VMEM((2, owners, windows, LANES), f32),
            pltpu.VMEM((2, owners, LANES), f32),
            pltpu.VMEM((owners * receivers, bins), bf16),
            pltpu.VMEM(shape, f32),
            pltpu.SemaphoreType.DMA((PIECES,)),
        ],
        compiler_params=pltpu.CompilerParams(vmem_limit_bytes=24 << 20),
        cost_estimate=pl.CostEstimate(flops=5 * 10**9, bytes_accessed=10 << 20, transcendentals=0),
        name="correlate",
    )(keep, held_spectra, *totals[1], gots[1], jnp.asarray(table[bins:]), part)


def solution(mesh):
    in_specs = (
        P(("groups", "chan"), None, None),
        P(("groups", "chan")),
        P(("groups", "chan")),
        P(("groups", "chan")),
    )
    out_specs = P(None, ("groups", "chan"), None)
    return jax.shard_map(shards, mesh=mesh, in_specs=in_specs, out_specs=out_specs, check_vma=False)
```

```python
import functools
import math

import jax
import jax.numpy as jnp
import ml_dtypes
import numpy as np
from jax import lax
from jax.experimental import pallas as pl
from jax.experimental.pallas import tpu as pltpu
from jax.sharding import PartitionSpec as P

NFFT = 12000
LAGW = 1024
SMOOTH = 64
LANES = 128
UNROLL = 4
PIECES = 4
BEGIN = 3 * 10**9
VMEM = pl.BlockSpec(memory_space=pltpu.VMEM)
SMEM = pl.BlockSpec(memory_space=pltpu.SMEM)
HBM = pl.BlockSpec(memory_space=pltpu.HBM)
f32 = jnp.float32
bf16 = jnp.bfloat16


def lag_table(bins):
    k = np.arange(1, bins + 1, dtype=np.int64)
    angle = 2.0 * np.pi / NFFT * np.mod(k[:, None] * np.arange(LAGW)[None, :], NFFT)
    both = np.stack([np.cos(angle), -np.sin(angle)]).reshape(2, bins // LANES, LANES, LAGW)
    return both.transpose(1, 0, 2, 3).reshape(2 * bins, LAGW).astype(ml_dtypes.bfloat16)


def orders(owners):
    bits = [1 << i for i in range(owners.bit_length() - 1)]
    near, far = bits[1:], bits[:0:-1]
    totals = near[1::-1] + near[2:], near[-1:] + near[:-1]
    return totals, (far + [1], far[-1:] + far[:-1] + [1])


def masks(order):
    out = [0]
    for bit in order:
        out = out + [m ^ bit for m in out]
    return out


def swap(value, bit):
    owners = lax.axis_size("chan")
    return lax.ppermute(value, "chan", [(i, i ^ bit) for i in range(owners)])


def pick_rows(bins, source_pick, lag_start, bad_flag, spectra, first, second, keeps, flags, sems):
    half = bins // 2
    pick, lag = source_pick[0], lag_start[0]
    copies = [pltpu.make_async_copy(bad_flag, flags, sems.at[4])]
    for h, rows in enumerate((first, second)):
        for part in range(2):
            copies.append(
                pltpu.make_async_copy(
                    spectra.at[pick, :, pl.ds(part * bins + h * half, half)],
                    rows.at[0, :, pl.ds(part * half, half)],
                    sems.at[2 * h + part],
                )
            )
    for copy in copies:
        copy.start()
    row = lax.broadcasted_iota(jnp.int32, (spectra.shape[1], LANES), 0)
    high = lax.shift_right_arithmetic(lag, 5)
    low = lag - high * 32
    copies[0].wait()
    keep = (1 - flags[pick]).astype(f32)
    extra = jnp.where(row == 0, high.astype(f32), jnp.where(row == 1, low.astype(f32), keep))
    for rows in (first, second):
        rows[0, :, pl.ds(bins, LANES)] = extra.astype(bf16)
    for r in range(keeps.shape[0]):
        keeps[r] = jnp.full(keeps.shape[1:], (1 - flags[r]).astype(f32))
    for copy in copies[1:]:
        copy.wait()


def add_channels(bins, spectra, *outs):
    core = lax.axis_index("chan") & 1
    half = bins // 2
    outs[4][...] = spectra[...]
    for h in range(2):
        own, other = outs[2 * h : 2 * h + 2]
        for part in range(2):
            src = pl.ds(part * bins + h * half, half)
            total = spectra[0, :, src].astype(f32)
            for r in range(1, spectra.shape[0]):
                total = total + spectra[r, :, src].astype(f32)

            @pl.when(core == part)
            def _():
                own[...] = total

            @pl.when(core != part)
            def _():
                other[...] = total


def cos_sin(turns):
    whole = jnp.floor(turns * (1.0 / NFFT) + 0.5)
    rest = turns - whole * NFFT
    quarter = jnp.floor(rest * (4.0 / NFFT) + 0.5)
    phi = (rest - quarter * (NFFT / 4)) * (2.0 * math.pi / NFFT)
    sq = phi * phi
    s = phi * (1.0 + sq * (-1 / 6 + sq * (1 / 120 + sq * (-1 / 5040))))
    c = 1.0 + sq * (-0.5 + sq * (1 / 24 + sq * (-1 / 720 + sq * (1 / 40320))))
    swapped = jnp.abs(quarter) == 1.0
    cos_neg = (quarter == 1.0) | (jnp.abs(quarter) == 2.0)
    sin_neg = (quarter == -1.0) | (jnp.abs(quarter) == 2.0)
    cosine = jnp.where(swapped, s, c)
    sine = jnp.where(swapped, c, s)
    return jnp.where(cos_neg, -cosine, cosine), jnp.where(sin_neg, -sine, sine)


def rounded(value):
    return value.astype(bf16).astype(f32)


def whitening(h, bins, channels, core, own, other, windows):
    half = bins // 2
    block_i = lax.broadcasted_iota(jnp.int32, (LANES, LANES), 0) // SMOOTH
    block_j = lax.broadcasted_iota(jnp.int32, (LANES, LANES), 1) // SMOOTH
    same = jnp.where(block_i == block_j, 1.0 / SMOOTH, 0.0).astype(bf16)
    lane = lax.broadcasted_iota(jnp.int32, (1, LANES), 1)
    inv = 1.0 / channels

    def means(c):
        at = pl.ds(pl.multiple_of(c * LANES, LANES), LANES)
        m_own, m_other = own[:, at] * inv, other[:, at] * inv
        return jnp.where(core == 0, m_own, m_other), jnp.where(core == 0, m_other, m_own)

    def scales(power):
        count = power.shape[0]
        power = power.reshape(count * windows, LANES)
        high = power.astype(bf16)
        low = (power - high.astype(f32)).astype(bf16)
        level = jnp.dot(high, same, preferred_element_type=f32) + jnp.dot(
            low, same, preferred_element_type=f32
        )
        return lax.rsqrt(level + 1e-6).reshape(count, windows, LANES)

    def numbers(c):
        return (lane + (h * half + 1) + c * LANES).astype(f32)

    return means, scales, numbers


def cross_rows(c, half, mean, scales, number, got, first, lags, kept, ang, src, receivers, a, b, pairs, norm, store):
    windows = got.shape[1]
    count = got.shape[0] - first
    re_at = pl.ds(pl.multiple_of(c * LANES, LANES), LANES)
    im_at = pl.ds(pl.multiple_of(half + c * LANES, LANES), LANES)
    cosine, sine = cos_sin(lags * number)
    ang[0], ang[1] = cosine * kept, sine * kept
    g_re = got[first:, :, re_at].astype(f32) - mean[0][None]
    g_im = got[first:, :, im_at].astype(f32) - mean[1][None]
    scale = scales(g_re * g_re + g_im * g_im)
    for i in range(count):
        w_re = rounded(g_re[i] * scale[i])
        w_im = rounded(g_im[i] * scale[i])
        cosine = ang[0, pl.ds(i, windows, stride=0), :]
        sine = ang[1, pl.ds(i, windows, stride=0), :]
        src[0, i] = rounded(w_re * cosine + w_im * sine)
        src[1, i] = rounded(w_im * cosine - w_re * sine)
    for row, members in pairs:
        pair = []
        for i in members:
            c_re = c_im = None
            for w in range(windows):
                g = src[0, i - first, pl.ds(w, receivers, stride=0), :]
                e = src[1, i - first, pl.ds(w, receivers, stride=0), :]
                t_re = g * a[w] + e * b[w]
                t_im = g * b[w] - e * a[w]
                c_re = t_re if c_re is None else c_re + t_re
                c_im = t_im if c_im is None else c_im + t_im
            pair.append((c_re * norm, c_im * norm))
        for part in range(2):
            cols = pl.ds(pl.multiple_of((2 * c + part) * LANES, LANES), LANES)
            both = jnp.concatenate([pair[0][part], pair[1][part]], 0)
            store[row : row + 2 * receivers, cols] = both.astype(bf16)


def correlate(h, bins, order, first_order, channels, keep, spectra, own, other, got, table, *rest):
    before, (out, rec, src, ang, cross, *leaving) = rest[:h], rest[h:]
    me = lax.axis_index("chan").astype(jnp.int32)
    core = me & 1
    receivers, windows = spectra.shape[0], spectra.shape[1]
    sources = got.shape[0]
    half = bins // 2
    chunks = half // LANES
    norm = 1.0 / math.sqrt(windows * bins)
    block_i = lax.broadcasted_iota(jnp.int32, (LANES, LANES), 0) // SMOOTH
    block_j = lax.broadcasted_iota(jnp.int32, (LANES, LANES), 1) // SMOOTH
    same = jnp.where(block_i == block_j, 1.0 / SMOOTH, 0.0).astype(bf16)
    lane = lax.broadcasted_iota(jnp.int32, (1, LANES), 1)
    inv = 1.0 / channels
    places, seen = masks(first_order), masks(order)
    held = [seen.index(m) for m in places]
    tail = got[:, :, pl.ds(bins, LANES)].astype(f32)
    lags = tail[:, 0, :] * 32.0 + tail[:, 1, :]
    kept = tail[:, 2, :]

    def scales(power):
        count = power.shape[0]
        power = power.reshape(count * windows, LANES)
        high = power.astype(bf16)
        low = (power - high.astype(f32)).astype(bf16)
        level = jnp.dot(high, same, preferred_element_type=f32) + jnp.dot(
            low, same, preferred_element_type=f32
        )
        return lax.rsqrt(level + 1e-6).reshape(count, windows, LANES)

    def chunk(c, _):
        re_at = pl.ds(pl.multiple_of(c * LANES, LANES), LANES)
        im_at = pl.ds(pl.multiple_of(half + c * LANES, LANES), LANES)
        bin_at = pl.ds(pl.multiple_of(h * half + c * LANES, LANES), LANES)
        imag_at = pl.ds(pl.multiple_of(bins + h * half + c * LANES, LANES), LANES)
        m_own, m_other = own[:, re_at] * inv, other[:, re_at] * inv
        m_re = jnp.where(core == 0, m_own, m_other)
        m_im = jnp.where(core == 0, m_other, m_own)
        x_re = spectra[:, :, bin_at].astype(f32) - m_re[None]
        x_im = spectra[:, :, imag_at].astype(f32) - m_im[None]
        scale = scales(x_re * x_re + x_im * x_im)
        for r in range(receivers):
            factor = scale[r] * keep[r]
            rec[0, r] = rounded(x_re[r] * factor)
            rec[1, r] = rounded(x_im[r] * factor)
        k = (lane + (h * half + 1) + c * LANES).astype(f32)
        cosine, sine = cos_sin(lags * k)
        ang[0], ang[1] = cosine * kept, sine * kept
        g_re = got[:, :, re_at].astype(f32) - m_re[None]
        g_im = got[:, :, im_at].astype(f32) - m_im[None]
        scale = scales(g_re * g_re + g_im * g_im)
        for i in range(sources):
            w_re = rounded(g_re[i] * scale[i])
            w_im = rounded(g_im[i] * scale[i])
            cosine = ang[0, pl.ds(i, windows, stride=0), :]
            sine = ang[1, pl.ds(i, windows, stride=0), :]
            src[0, i] = rounded(w_re * cosine + w_im * sine)
            src[1, i] = rounded(w_im * cosine - w_re * sine)
        a = [rec[0, :, w, :] for w in range(windows)]
        b = [rec[1, :, w, :] for w in range(windows)]
        for p in range(0, sources, 2):
            pair = []
            for i in (held[p], held[p + 1]):
                c_re = c_im = None
                for w in range(windows):
                    g = src[0, i, pl.ds(w, receivers, stride=0), :]
                    e = src[1, i, pl.ds(w, receivers, stride=0), :]
                    t_re = g * a[w] + e * b[w]
                    t_im = g * b[w] - e * a[w]
                    c_re = t_re if c_re is None else c_re + t_re
                    c_im = t_im if c_im is None else c_im + t_im
                pair.append((c_re * norm, c_im * norm))
            for part in range(2):
                cols = pl.ds(pl.multiple_of((2 * c + part) * LANES, LANES), LANES)
                both = jnp.concatenate([pair[0][part], pair[1][part]], 0)
                cross[p * receivers : (p + 2) * receivers, cols] = both.astype(bf16)
        return 0

    lax.fori_loop(0, chunks, chunk, 0, unroll=UNROLL)
    if h == 0:
        out[...] = jnp.dot(cross[...], table[...], preferred_element_type=f32)
        return
    final, sems = leaving
    copies = []
    for piece in range(PIECES):
        cols = slice(piece * LAGW // PIECES, (piece + 1) * LAGW // PIECES)
        product = before[0][:, cols] + jnp.dot(
            cross[...], table[:, cols], preferred_element_type=f32
        )
        for p in range(sources):
            source = jnp.bitwise_xor(me, places[p])
            final[source, :, cols] = product[p * receivers : (p + 1) * receivers, :]
        copies.append(
            pltpu.make_async_copy(final.at[:, :, cols], out.at[:, :, cols], sems.at[piece])
        )
        copies[-1].start()
    for copy in copies:
        copy.wait()


def begin(h, bins, pairs, channels, keep, spectra, own, other, got, white, store, src, ang):
    core = lax.axis_index("chan") & 1
    receivers, windows = spectra.shape[0], spectra.shape[1]
    half = bins // 2
    norm = 1.0 / math.sqrt(windows * bins)
    means, scales, numbers = whitening(h, bins, channels, core, own, other, windows)
    tail = got[:, :, pl.ds(bins, LANES)].astype(f32)
    lags, kept = tail[:, 0, :] * 32.0 + tail[:, 1, :], tail[:, 2, :]

    def chunk(c, _):
        bin_at = pl.ds(pl.multiple_of(h * half + c * LANES, LANES), LANES)
        imag_at = pl.ds(pl.multiple_of(bins + h * half + c * LANES, LANES), LANES)
        mean = means(c)
        x_re = spectra[:, :, bin_at].astype(f32) - mean[0][None]
        x_im = spectra[:, :, imag_at].astype(f32) - mean[1][None]
        scale = scales(x_re * x_re + x_im * x_im)
        for r in range(receivers):
            factor = scale[r] * keep[r]
            white[c, 0, r] = rounded(x_re[r] * factor)
            white[c, 1, r] = rounded(x_im[r] * factor)
        a = [white[c, 0, :, w, :] for w in range(windows)]
        b = [white[c, 1, :, w, :] for w in range(windows)]
        cross_rows(
            c, half, mean, scales, numbers(c), got, 0, lags, kept, ang, src, receivers, a, b, pairs, norm, store
        )
        return 0

    lax.fori_loop(0, half // LANES, chunk, 0, unroll=UNROLL)


def finish(h, bins, first, early, pairs, places, channels, own, other, got, white, store, table, *rest):
    before, (out, src, ang, cross, *leaving) = rest[:h], rest[h:]
    me = lax.axis_index("chan").astype(jnp.int32)
    core = me & 1
    receivers, windows = white.shape[2], white.shape[3]
    half = bins // 2
    norm = 1.0 / math.sqrt(windows * bins)
    means, scales, numbers = whitening(h, bins, channels, core, own, other, windows)
    tail = got[first:, :, pl.ds(bins, LANES)].astype(f32)
    lags, kept = tail[:, 0, :] * 32.0 + tail[:, 1, :], tail[:, 2, :]
    for source, dest in early:
        cross[dest : dest + 2 * receivers, :] = store[source : source + 2 * receivers, :]

    def chunk(c, _):
        a = [white[c, 0, :, w, :] for w in range(windows)]
        b = [white[c, 1, :, w, :] for w in range(windows)]
        cross_rows(
            c, half, means(c), scales, numbers(c), got, first, lags, kept, ang, src, receivers, a, b, pairs, norm,
            cross,
        )
        return 0

    lax.fori_loop(0, half // LANES, chunk, 0, unroll=UNROLL)
    if h == 0:
        out[...] = jnp.dot(cross[...], table[...], preferred_element_type=f32)
        return
    final, sems = leaving
    copies = []
    for piece in range(PIECES):
        cols = slice(piece * LAGW // PIECES, (piece + 1) * LAGW // PIECES)
        product = before[0][:, cols] + jnp.dot(
            cross[...], table[:, cols], preferred_element_type=f32
        )
        for p, place in enumerate(places):
            source = jnp.bitwise_xor(me, place)
            final[source, :, cols] = product[p * receivers : (p + 1) * receivers, :]
        copies.append(
            pltpu.make_async_copy(final.at[:, :, cols], out.at[:, :, cols], sems.at[piece])
        )
        copies[-1].start()
    for copy in copies:
        copy.wait()


def shards(spectra, bad_flag, source_pick, lag_start):
    receivers, windows, width_both = spectra.shape
    bins = width_both // 2
    owners = lax.axis_size("chan")
    half = bins // 2
    flat = jax.ShapeDtypeStruct((windows, half), f32)
    rows = jax.ShapeDtypeStruct((1, windows, bins + LANES), bf16)
    first, second, keep = pl.pallas_call(
        functools.partial(pick_rows, bins),
        out_shape=(rows, rows, jax.ShapeDtypeStruct((receivers, windows, LANES), f32)),
        in_specs=[SMEM, SMEM, HBM, HBM],
        out_specs=(VMEM,) * 3,
        scratch_shapes=[pltpu.SMEM((receivers,), jnp.int32), pltpu.SemaphoreType.DMA((5,))],
        compiler_params=pltpu.CompilerParams(vmem_limit_bytes=8 << 20),
        name="pick_rows",
    )(
        source_pick,
        lag_start,
        pltpu.with_memory_space_constraint(bad_flag, pltpu.HBM),
        pltpu.with_memory_space_constraint(spectra, pltpu.HBM),
    )
    sums = pl.pallas_call(
        functools.partial(add_channels, bins),
        out_shape=(flat,) * 4 + (jax.ShapeDtypeStruct(spectra.shape, bf16),),
        in_specs=[VMEM],
        out_specs=(VMEM,) * 5,
        compiler_params=pltpu.CompilerParams(vmem_limit_bytes=8 << 20),
        name="add_channels",
    )(spectra)
    held_spectra = sums[4]
    total_order, row_order = orders(owners)
    table = lag_table(bins)
    channels = receivers * owners
    chunks = half // LANES
    first_count = owners // 4
    places = masks(row_order[0])
    totals, gots, begun = [], [], []
    for h in range(2):
        own, other = sums[2 * h : 2 * h + 2]
        got = (first, second)[h]
        total = own + swap(other, 1)
        for bit in total_order[h]:
            total = total + swap(total, bit)
        totals.append((total, swap(total, 1)))
        held = [masks(row_order[h]).index(m) for m in places]
        pairs = [(p * receivers, (held[p], held[p + 1])) for p in range(0, owners, 2)]
        early = [pair for pair in pairs if max(pair[1]) < first_count]
        late = [pair for pair in pairs if max(pair[1]) >= first_count]
        moved = [(2 * receivers * i, row) for i, (row, _) in enumerate(early)]
        for bit in row_order[h]:
            if h == 0 and got.shape[0] == first_count:
                begun.append(
                    (moved, late)
                    + tuple(
                        pl.pallas_call(
                            functools.partial(
                                begin, h, bins, [(2 * receivers * i, m) for i, (_, m) in enumerate(early)], channels
                            ),
                            out_shape=(
                                jax.ShapeDtypeStruct((chunks, 2, receivers, windows, LANES), f32),
                                jax.ShapeDtypeStruct((first_count * receivers, bins), bf16),
                            ),
                            in_specs=[VMEM] * 5,
                            out_specs=(VMEM, VMEM),
                            scratch_shapes=[
                                pltpu.VMEM((2, first_count, windows, LANES), f32),
                                pltpu.VMEM((2, first_count, LANES), f32),
                            ],
                            compiler_params=pltpu.CompilerParams(vmem_limit_bytes=16 << 20),
                            cost_estimate=pl.CostEstimate(flops=BEGIN, bytes_accessed=4 << 20, transcendentals=0),
                            name="begin",
                        )(keep, held_spectra, *totals[h], got)
                    )
                )
            got = jnp.concatenate([got, swap(got, bit)], 0)
        gots.append(got)
    late_count = owners - first_count
    whole = (owners * receivers, LAGW)
    moved, late, white, store = begun[0]
    part = pl.pallas_call(
        functools.partial(finish, 0, bins, first_count, moved, late, places, channels),
        out_shape=jax.ShapeDtypeStruct(whole, f32),
        in_specs=[VMEM] * 6,
        out_specs=VMEM,
        scratch_shapes=[
            pltpu.VMEM((2, late_count, windows, LANES), f32),
            pltpu.VMEM((2, late_count, LANES), f32),
            pltpu.VMEM((owners * receivers, bins), bf16),
        ],
        compiler_params=pltpu.CompilerParams(vmem_limit_bytes=16 << 20),
        cost_estimate=pl.CostEstimate(flops=4 * 10**9, bytes_accessed=10 << 20, transcendentals=0),
        name="finish",
    )(*totals[0], gots[0], white, store, jnp.asarray(table[:bins]))
    shape = (owners, receivers, LAGW)
    return pl.pallas_call(
        functools.partial(correlate, 1, bins, row_order[1], row_order[0], channels),
        out_shape=jax.ShapeDtypeStruct(shape, f32),
        in_specs=[VMEM] * 7,
        out_specs=HBM,
        scratch_shapes=[
            pltpu.VMEM((2, receivers, windows, LANES), f32),
            pltpu.VMEM((2, owners, windows, LANES), f32),
            pltpu.VMEM((2, owners, LANES), f32),
            pltpu.VMEM((owners * receivers, bins), bf16),
            pltpu.VMEM(shape, f32),
            pltpu.SemaphoreType.DMA((PIECES,)),
        ],
        compiler_params=pltpu.CompilerParams(vmem_limit_bytes=24 << 20),
        cost_estimate=pl.CostEstimate(flops=5 * 10**9, bytes_accessed=10 << 20, transcendentals=0),
        name="correlate",
    )(keep, held_spectra, *totals[1], gots[1], jnp.asarray(table[bins:]), part)


def solution(mesh):
    in_specs = (
        P(("groups", "chan"), None, None),
        P(("groups", "chan")),
        P(("groups", "chan")),
        P(("groups", "chan")),
    )
    out_specs = P(None, ("groups", "chan"), None)
    return jax.shard_map(shards, mesh=mesh, in_specs=in_specs, out_specs=out_specs, check_vma=False)
```

```python
import functools
import math

import jax
import jax.numpy as jnp
import ml_dtypes
import numpy as np
from jax import lax
from jax.experimental import pallas as pl
from jax.experimental.pallas import tpu as pltpu
from jax.sharding import PartitionSpec as P

NFFT = 12000
LAGW = 1024
SMOOTH = 64
LANES = 128
UNROLL = 6
PIECES = 4
BEGIN = 3 * 10**9
VMEM = pl.BlockSpec(memory_space=pltpu.VMEM)
SMEM = pl.BlockSpec(memory_space=pltpu.SMEM)
HBM = pl.BlockSpec(memory_space=pltpu.HBM)
f32 = jnp.float32
bf16 = jnp.bfloat16


def lag_table(bins):
    k = np.arange(1, bins + 1, dtype=np.int64)
    angle = 2.0 * np.pi / NFFT * np.mod(k[:, None] * np.arange(LAGW)[None, :], NFFT)
    both = np.stack([np.cos(angle), -np.sin(angle)]).reshape(2, bins // LANES, LANES, LAGW)
    return both.transpose(1, 0, 2, 3).reshape(2 * bins, LAGW).astype(ml_dtypes.bfloat16)


def orders(owners):
    bits = [1 << i for i in range(owners.bit_length() - 1)]
    near, far = bits[1:], bits[:0:-1]
    totals = near[1::-1] + near[2:], near[-1:] + near[:-1]
    return totals, (far + [1], far[-1:] + far[:-1] + [1])


def masks(order):
    out = [0]
    for bit in order:
        out = out + [m ^ bit for m in out]
    return out


def swap(value, bit):
    owners = lax.axis_size("chan")
    return lax.ppermute(value, "chan", [(i, i ^ bit) for i in range(owners)])


def pick_rows(bins, source_pick, lag_start, bad_flag, spectra, first, second, keeps, flags, sems):
    half = bins // 2
    pick, lag = source_pick[0], lag_start[0]
    copies = [pltpu.make_async_copy(bad_flag, flags, sems.at[4])]
    for h, rows in enumerate((first, second)):
        for part in range(2):
            copies.append(
                pltpu.make_async_copy(
                    spectra.at[pick, :, pl.ds(part * bins + h * half, half)],
                    rows.at[0, :, pl.ds(part * half, half)],
                    sems.at[2 * h + part],
                )
            )
    for copy in copies:
        copy.start()
    row = lax.broadcasted_iota(jnp.int32, (spectra.shape[1], LANES), 0)
    high = lax.shift_right_arithmetic(lag, 5)
    low = lag - high * 32
    copies[0].wait()
    keep = (1 - flags[pick]).astype(f32)
    extra = jnp.where(row == 0, high.astype(f32), jnp.where(row == 1, low.astype(f32), keep))
    for rows in (first, second):
        rows[0, :, pl.ds(bins, LANES)] = extra.astype(bf16)
    for r in range(keeps.shape[0]):
        keeps[r] = jnp.full(keeps.shape[1:], (1 - flags[r]).astype(f32))
    for copy in copies[1:]:
        copy.wait()


def add_channels(bins, spectra, *outs):
    core = lax.axis_index("chan") & 1
    half = bins // 2
    outs[4][...] = spectra[...]
    for h in range(2):
        own, other = outs[2 * h : 2 * h + 2]
        for part in range(2):
            src = pl.ds(part * bins + h * half, half)
            total = spectra[0, :, src].astype(f32)
            for r in range(1, spectra.shape[0]):
                total = total + spectra[r, :, src].astype(f32)

            @pl.when(core == part)
            def _():
                own[...] = total

            @pl.when(core != part)
            def _():
                other[...] = total


def cos_sin(turns):
    whole = jnp.floor(turns * (1.0 / NFFT) + 0.5)
    rest = turns - whole * NFFT
    quarter = jnp.floor(rest * (4.0 / NFFT) + 0.5)
    phi = (rest - quarter * (NFFT / 4)) * (2.0 * math.pi / NFFT)
    sq = phi * phi
    s = phi * (1.0 + sq * (-1 / 6 + sq * (1 / 120 + sq * (-1 / 5040))))
    c = 1.0 + sq * (-0.5 + sq * (1 / 24 + sq * (-1 / 720 + sq * (1 / 40320))))
    swapped = jnp.abs(quarter) == 1.0
    cos_neg = (quarter == 1.0) | (jnp.abs(quarter) == 2.0)
    sin_neg = (quarter == -1.0) | (jnp.abs(quarter) == 2.0)
    cosine = jnp.where(swapped, s, c)
    sine = jnp.where(swapped, c, s)
    return jnp.where(cos_neg, -cosine, cosine), jnp.where(sin_neg, -sine, sine)


def rounded(value):
    return value.astype(bf16).astype(f32)


def whitening(h, bins, channels, core, own, other, windows):
    half = bins // 2
    block_i = lax.broadcasted_iota(jnp.int32, (LANES, LANES), 0) // SMOOTH
    block_j = lax.broadcasted_iota(jnp.int32, (LANES, LANES), 1) // SMOOTH
    same = jnp.where(block_i == block_j, 1.0 / SMOOTH, 0.0).astype(bf16)
    lane = lax.broadcasted_iota(jnp.int32, (1, LANES), 1)
    inv = 1.0 / channels

    def means(c):
        at = pl.ds(pl.multiple_of(c * LANES, LANES), LANES)
        m_own, m_other = own[:, at] * inv, other[:, at] * inv
        return jnp.where(core == 0, m_own, m_other), jnp.where(core == 0, m_other, m_own)

    def scales(power):
        count = power.shape[0]
        power = power.reshape(count * windows, LANES)
        high = power.astype(bf16)
        low = (power - high.astype(f32)).astype(bf16)
        level = jnp.dot(high, same, preferred_element_type=f32) + jnp.dot(
            low, same, preferred_element_type=f32
        )
        return lax.rsqrt(level + 1e-6).reshape(count, windows, LANES)

    def numbers(c):
        return (lane + (h * half + 1) + c * LANES).astype(f32)

    return means, scales, numbers


def cross_rows(c, half, mean, scales, number, got, first, lags, kept, ang, src, receivers, a, b, pairs, norm, store):
    windows = got.shape[1]
    count = got.shape[0] - first
    re_at = pl.ds(pl.multiple_of(c * LANES, LANES), LANES)
    im_at = pl.ds(pl.multiple_of(half + c * LANES, LANES), LANES)
    cosine, sine = cos_sin(lags * number)
    ang[0], ang[1] = cosine * kept, sine * kept
    g_re = got[first:, :, re_at].astype(f32) - mean[0][None]
    g_im = got[first:, :, im_at].astype(f32) - mean[1][None]
    scale = scales(g_re * g_re + g_im * g_im)
    for i in range(count):
        w_re = rounded(g_re[i] * scale[i])
        w_im = rounded(g_im[i] * scale[i])
        cosine = ang[0, pl.ds(i, windows, stride=0), :]
        sine = ang[1, pl.ds(i, windows, stride=0), :]
        src[0, i] = rounded(w_re * cosine + w_im * sine)
        src[1, i] = rounded(w_im * cosine - w_re * sine)
    for row, members in pairs:
        pair = []
        for i in members:
            c_re = c_im = None
            for w in range(windows):
                g = src[0, i - first, pl.ds(w, receivers, stride=0), :]
                e = src[1, i - first, pl.ds(w, receivers, stride=0), :]
                t_re = g * a[w] + e * b[w]
                t_im = g * b[w] - e * a[w]
                c_re = t_re if c_re is None else c_re + t_re
                c_im = t_im if c_im is None else c_im + t_im
            pair.append((c_re * norm, c_im * norm))
        for part in range(2):
            cols = pl.ds(pl.multiple_of((2 * c + part) * LANES, LANES), LANES)
            both = jnp.concatenate([pair[0][part], pair[1][part]], 0)
            store[row : row + 2 * receivers, cols] = both.astype(bf16)


def correlate(h, bins, order, first_order, channels, keep, spectra, own, other, got, table, *rest):
    before, (out, rec, src, ang, cross, *leaving) = rest[:h], rest[h:]
    me = lax.axis_index("chan").astype(jnp.int32)
    core = me & 1
    receivers, windows = spectra.shape[0], spectra.shape[1]
    sources = got.shape[0]
    half = bins // 2
    chunks = half // LANES
    norm = 1.0 / math.sqrt(windows * bins)
    block_i = lax.broadcasted_iota(jnp.int32, (LANES, LANES), 0) // SMOOTH
    block_j = lax.broadcasted_iota(jnp.int32, (LANES, LANES), 1) // SMOOTH
    same = jnp.where(block_i == block_j, 1.0 / SMOOTH, 0.0).astype(bf16)
    lane = lax.broadcasted_iota(jnp.int32, (1, LANES), 1)
    inv = 1.0 / channels
    places, seen = masks(first_order), masks(order)
    held = [seen.index(m) for m in places]
    tail = got[:, :, pl.ds(bins, LANES)].astype(f32)
    lags = tail[:, 0, :] * 32.0 + tail[:, 1, :]
    kept = tail[:, 2, :]

    def scales(power):
        count = power.shape[0]
        power = power.reshape(count * windows, LANES)
        high = power.astype(bf16)
        low = (power - high.astype(f32)).astype(bf16)
        level = jnp.dot(high, same, preferred_element_type=f32) + jnp.dot(
            low, same, preferred_element_type=f32
        )
        return lax.rsqrt(level + 1e-6).reshape(count, windows, LANES)

    def chunk(c, _):
        re_at = pl.ds(pl.multiple_of(c * LANES, LANES), LANES)
        im_at = pl.ds(pl.multiple_of(half + c * LANES, LANES), LANES)
        bin_at = pl.ds(pl.multiple_of(h * half + c * LANES, LANES), LANES)
        imag_at = pl.ds(pl.multiple_of(bins + h * half + c * LANES, LANES), LANES)
        m_own, m_other = own[:, re_at] * inv, other[:, re_at] * inv
        m_re = jnp.where(core == 0, m_own, m_other)
        m_im = jnp.where(core == 0, m_other, m_own)
        x_re = spectra[:, :, bin_at].astype(f32) - m_re[None]
        x_im = spectra[:, :, imag_at].astype(f32) - m_im[None]
        scale = scales(x_re * x_re + x_im * x_im)
        for r in range(receivers):
            factor = scale[r] * keep[r]
            rec[0, r] = rounded(x_re[r] * factor)
            rec[1, r] = rounded(x_im[r] * factor)
        k = (lane + (h * half + 1) + c * LANES).astype(f32)
        cosine, sine = cos_sin(lags * k)
        ang[0], ang[1] = cosine * kept, sine * kept
        g_re = got[:, :, re_at].astype(f32) - m_re[None]
        g_im = got[:, :, im_at].astype(f32) - m_im[None]
        scale = scales(g_re * g_re + g_im * g_im)
        for i in range(sources):
            w_re = rounded(g_re[i] * scale[i])
            w_im = rounded(g_im[i] * scale[i])
            cosine = ang[0, pl.ds(i, windows, stride=0), :]
            sine = ang[1, pl.ds(i, windows, stride=0), :]
            src[0, i] = rounded(w_re * cosine + w_im * sine)
            src[1, i] = rounded(w_im * cosine - w_re * sine)
        a = [rec[0, :, w, :] for w in range(windows)]
        b = [rec[1, :, w, :] for w in range(windows)]
        for p in range(0, sources, 2):
            pair = []
            for i in (held[p], held[p + 1]):
                c_re = c_im = None
                for w in range(windows):
                    g = src[0, i, pl.ds(w, receivers, stride=0), :]
                    e = src[1, i, pl.ds(w, receivers, stride=0), :]
                    t_re = g * a[w] + e * b[w]
                    t_im = g * b[w] - e * a[w]
                    c_re = t_re if c_re is None else c_re + t_re
                    c_im = t_im if c_im is None else c_im + t_im
                pair.append((c_re * norm, c_im * norm))
            for part in range(2):
                cols = pl.ds(pl.multiple_of((2 * c + part) * LANES, LANES), LANES)
                both = jnp.concatenate([pair[0][part], pair[1][part]], 0)
                cross[p * receivers : (p + 2) * receivers, cols] = both.astype(bf16)
        return 0

    lax.fori_loop(0, chunks, chunk, 0, unroll=UNROLL)
    if h == 0:
        out[...] = jnp.dot(cross[...], table[...], preferred_element_type=f32)
        return
    final, sems = leaving
    copies = []
    for piece in range(PIECES):
        cols = slice(piece * LAGW // PIECES, (piece + 1) * LAGW // PIECES)
        product = before[0][:, cols] + jnp.dot(
            cross[...], table[:, cols], preferred_element_type=f32
        )
        for p in range(sources):
            source = jnp.bitwise_xor(me, places[p])
            final[source, :, cols] = product[p * receivers : (p + 1) * receivers, :]
        copies.append(
            pltpu.make_async_copy(final.at[:, :, cols], out.at[:, :, cols], sems.at[piece])
        )
        copies[-1].start()
    for copy in copies:
        copy.wait()


def begin(h, bins, pairs, channels, keep, spectra, own, other, got, white, store, src, ang):
    core = lax.axis_index("chan") & 1
    receivers, windows = spectra.shape[0], spectra.shape[1]
    half = bins // 2
    norm = 1.0 / math.sqrt(windows * bins)
    means, scales, numbers = whitening(h, bins, channels, core, own, other, windows)
    tail = got[:, :, pl.ds(bins, LANES)].astype(f32)
    lags, kept = tail[:, 0, :] * 32.0 + tail[:, 1, :], tail[:, 2, :]

    def chunk(c, _):
        bin_at = pl.ds(pl.multiple_of(h * half + c * LANES, LANES), LANES)
        imag_at = pl.ds(pl.multiple_of(bins + h * half + c * LANES, LANES), LANES)
        mean = means(c)
        x_re = spectra[:, :, bin_at].astype(f32) - mean[0][None]
        x_im = spectra[:, :, imag_at].astype(f32) - mean[1][None]
        scale = scales(x_re * x_re + x_im * x_im)
        for r in range(receivers):
            factor = scale[r] * keep[r]
            white[c, 0, r] = rounded(x_re[r] * factor)
            white[c, 1, r] = rounded(x_im[r] * factor)
        a = [white[c, 0, :, w, :] for w in range(windows)]
        b = [white[c, 1, :, w, :] for w in range(windows)]
        cross_rows(
            c, half, mean, scales, numbers(c), got, 0, lags, kept, ang, src, receivers, a, b, pairs, norm, store
        )
        return 0

    lax.fori_loop(0, half // LANES, chunk, 0, unroll=UNROLL)


def finish(h, bins, first, early, pairs, places, channels, own, other, got, white, store, table, *rest):
    before, (out, src, ang, cross, *leaving) = rest[:h], rest[h:]
    me = lax.axis_index("chan").astype(jnp.int32)
    core = me & 1
    receivers, windows = white.shape[2], white.shape[3]
    half = bins // 2
    norm = 1.0 / math.sqrt(windows * bins)
    means, scales, numbers = whitening(h, bins, channels, core, own, other, windows)
    tail = got[first:, :, pl.ds(bins, LANES)].astype(f32)
    lags, kept = tail[:, 0, :] * 32.0 + tail[:, 1, :], tail[:, 2, :]
    for source, dest in early:
        cross[dest : dest + 2 * receivers, :] = store[source : source + 2 * receivers, :]

    def chunk(c, _):
        a = [white[c, 0, :, w, :] for w in range(windows)]
        b = [white[c, 1, :, w, :] for w in range(windows)]
        cross_rows(
            c, half, means(c), scales, numbers(c), got, first, lags, kept, ang, src, receivers, a, b, pairs, norm,
            cross,
        )
        return 0

    lax.fori_loop(0, half // LANES, chunk, 0, unroll=UNROLL)
    if h == 0:
        out[...] = jnp.dot(cross[...], table[...], preferred_element_type=f32)
        return
    final, sems = leaving
    copies = []
    for piece in range(PIECES):
        cols = slice(piece * LAGW // PIECES, (piece + 1) * LAGW // PIECES)
        product = before[0][:, cols] + jnp.dot(
            cross[...], table[:, cols], preferred_element_type=f32
        )
        for p, place in enumerate(places):
            source = jnp.bitwise_xor(me, place)
            final[source, :, cols] = product[p * receivers : (p + 1) * receivers, :]
        copies.append(
            pltpu.make_async_copy(final.at[:, :, cols], out.at[:, :, cols], sems.at[piece])
        )
        copies[-1].start()
    for copy in copies:
        copy.wait()


def shards(spectra, bad_flag, source_pick, lag_start):
    receivers, windows, width_both = spectra.shape
    bins = width_both // 2
    owners = lax.axis_size("chan")
    half = bins // 2
    flat = jax.ShapeDtypeStruct((windows, half), f32)
    rows = jax.ShapeDtypeStruct((1, windows, bins + LANES), bf16)
    first, second, keep = pl.pallas_call(
        functools.partial(pick_rows, bins),
        out_shape=(rows, rows, jax.ShapeDtypeStruct((receivers, windows, LANES), f32)),
        in_specs=[SMEM, SMEM, HBM, HBM],
        out_specs=(VMEM,) * 3,
        scratch_shapes=[pltpu.SMEM((receivers,), jnp.int32), pltpu.SemaphoreType.DMA((5,))],
        compiler_params=pltpu.CompilerParams(vmem_limit_bytes=8 << 20),
        name="pick_rows",
    )(
        source_pick,
        lag_start,
        pltpu.with_memory_space_constraint(bad_flag, pltpu.HBM),
        pltpu.with_memory_space_constraint(spectra, pltpu.HBM),
    )
    sums = pl.pallas_call(
        functools.partial(add_channels, bins),
        out_shape=(flat,) * 4 + (jax.ShapeDtypeStruct(spectra.shape, bf16),),
        in_specs=[VMEM],
        out_specs=(VMEM,) * 5,
        compiler_params=pltpu.CompilerParams(vmem_limit_bytes=8 << 20),
        name="add_channels",
    )(spectra)
    held_spectra = sums[4]
    total_order, row_order = orders(owners)
    table = lag_table(bins)
    channels = receivers * owners
    chunks = half // LANES
    first_count = owners // 4
    places = masks(row_order[0])
    totals, gots, begun = [], [], []
    for h in range(2):
        own, other = sums[2 * h : 2 * h + 2]
        got = (first, second)[h]
        total = own + swap(other, 1)
        for bit in total_order[h]:
            total = total + swap(total, bit)
        totals.append((total, swap(total, 1)))
        held = [masks(row_order[h]).index(m) for m in places]
        pairs = [(p * receivers, (held[p], held[p + 1])) for p in range(0, owners, 2)]
        early = [pair for pair in pairs if max(pair[1]) < first_count]
        late = [pair for pair in pairs if max(pair[1]) >= first_count]
        moved = [(2 * receivers * i, row) for i, (row, _) in enumerate(early)]
        for bit in row_order[h]:
            if h == 0 and got.shape[0] == first_count:
                begun.append(
                    (moved, late)
                    + tuple(
                        pl.pallas_call(
                            functools.partial(
                                begin, h, bins, [(2 * receivers * i, m) for i, (_, m) in enumerate(early)], channels
                            ),
                            out_shape=(
                                jax.ShapeDtypeStruct((chunks, 2, receivers, windows, LANES), f32),
                                jax.ShapeDtypeStruct((first_count * receivers, bins), bf16),
                            ),
                            in_specs=[VMEM] * 5,
                            out_specs=(VMEM, VMEM),
                            scratch_shapes=[
                                pltpu.VMEM((2, first_count, windows, LANES), f32),
                                pltpu.VMEM((2, first_count, LANES), f32),
                            ],
                            compiler_params=pltpu.CompilerParams(vmem_limit_bytes=16 << 20),
                            cost_estimate=pl.CostEstimate(flops=BEGIN, bytes_accessed=4 << 20, transcendentals=0),
                            name="begin",
                        )(keep, held_spectra, *totals[h], got)
                    )
                )
            got = jnp.concatenate([got, swap(got, bit)], 0)
        gots.append(got)
    late_count = owners - first_count
    whole = (owners * receivers, LAGW)
    moved, late, white, store = begun[0]
    part = pl.pallas_call(
        functools.partial(finish, 0, bins, first_count, moved, late, places, channels),
        out_shape=jax.ShapeDtypeStruct(whole, f32),
        in_specs=[VMEM] * 6,
        out_specs=VMEM,
        scratch_shapes=[
            pltpu.VMEM((2, late_count, windows, LANES), f32),
            pltpu.VMEM((2, late_count, LANES), f32),
            pltpu.VMEM((owners * receivers, bins), bf16),
        ],
        compiler_params=pltpu.CompilerParams(vmem_limit_bytes=16 << 20),
        cost_estimate=pl.CostEstimate(flops=4 * 10**9, bytes_accessed=10 << 20, transcendentals=0),
        name="finish",
    )(*totals[0], gots[0], white, store, jnp.asarray(table[:bins]))
    shape = (owners, receivers, LAGW)
    return pl.pallas_call(
        functools.partial(correlate, 1, bins, row_order[1], row_order[0], channels),
        out_shape=jax.ShapeDtypeStruct(shape, f32),
        in_specs=[VMEM] * 7,
        out_specs=HBM,
        scratch_shapes=[
            pltpu.VMEM((2, receivers, windows, LANES), f32),
            pltpu.VMEM((2, owners, windows, LANES), f32),
            pltpu.VMEM((2, owners, LANES), f32),
            pltpu.VMEM((owners * receivers, bins), bf16),
            pltpu.VMEM(shape, f32),
            pltpu.SemaphoreType.DMA((PIECES,)),
        ],
        compiler_params=pltpu.CompilerParams(vmem_limit_bytes=24 << 20),
        cost_estimate=pl.CostEstimate(flops=5 * 10**9, bytes_accessed=10 << 20, transcendentals=0),
        name="correlate",
    )(keep, held_spectra, *totals[1], gots[1], jnp.asarray(table[bins:]), part)


def solution(mesh):
    in_specs = (
        P(("groups", "chan"), None, None),
        P(("groups", "chan")),
        P(("groups", "chan")),
        P(("groups", "chan")),
    )
    out_specs = P(None, ("groups", "chan"), None)
    return jax.shard_map(shards, mesh=mesh, in_specs=in_specs, out_specs=out_specs, check_vma=False)
```
